256 devices in a mesh: row: 32 (over y, x, core), col: 8 (over z).
Axes of the slice: x: 4, y: 4, z: 8, core: 2. Of those that a mesh axis runs over, the one named last changes fastest.
Arguments:
- diag: float32 [4, 1024, 1024], P(None, 'row'), as said below
- panel_rows: float32 [64, 8, 64, 1024], P('row', None, None, 'col')
- panel_cols: float32 [8, 8, 64, 1024], P('col', None, 'row')
- trailing: float32 [64, 8, 8, 64, 1024], P('row', 'col')
- sketch: float32 [64, 1024], replicated, may hold values from -6 to 6
- panel_rank: int32 [64], P('row'), may hold values from 16 to 64
- col_rank: int32 [8], P('col'), may hold values from 16 to 64
- tile_rank: int32 [64, 8], P('row', 'col'), may hold values from 32 to 64
- keep_rank: int32 [64, 8], P('row', 'col'), may hold values from 8 to 32
Outputs:
- new_tiles: float32 [64, 8, 8, 64, 1024], P('row', 'col')
The draws below stay inside these ranges and needn't reach their ends.
Inputs may be any that keep to these rules, and one draw needn't show every extreme that they name: `keep_rank`: recompression ranks, never above the tile's rank. diag[0] is symmetric positive definite with smallest eigenvalue 0.5 or more; the tangents are symmetric.
All inputs are finite; a program needn't handle non-finite values.
Results may differ from the reference program's by a relative error of at most 0.0003.
Values sent between devices are 32-bit elements; how exact they have to be, the bound alone decides.
A program may use at most 192 MiB of HBM per device.

```python
import math
import jax
import jax.numpy as jnp
from jax import lax

NB = 1024
RMAX = 64
TROWS = 64
TCOLS = 8


def factor_draw(key, shape, v_scale):
    values = jax.random.normal(key, shape, jnp.float32)
    scales = jnp.where(jnp.arange(8) < 4, 1.0, v_scale).astype(jnp.float32)
    return values * scales[:, None, None]


def draw_panel_rows(key, part):
    return factor_draw(key, (TROWS, 8, RMAX, NB), 1.0 / 32.0)


def draw_panel_cols(key, part):
    return factor_draw(key, (TCOLS, 8, RMAX, NB), 1.0 / 32.0)


def draw_trailing(key, part):
    return factor_draw(key, (TROWS, TCOLS, 8, RMAX, NB), 1.0 / 8.0)


def draw_diag(key, part):
    point_key = jax.random.fold_in(key, 11)
    noise_key = jax.random.fold_in(key, 23)
    points = jax.random.uniform(point_key, (NB, 2), jnp.float32)
    variance = 16.0
    length_scale = 0.06
    noise = 0.05 * jax.random.normal(noise_key, (3, NB, NB), jnp.float32)
    noise = (noise + jnp.swapaxes(noise, 1, 2)) / math.sqrt(2.0)
    offsets = points[:, None, :] - points[None, :, :]
    distance = jnp.sqrt(jnp.sum(offsets * offsets, axis=-1))
    scaled = math.sqrt(3.0) * distance / length_scale
    kernel = (1.0 + scaled) * jnp.exp(-scaled)
    identity = jnp.eye(NB, dtype=jnp.float32)
    primal = variance * kernel + 0.5 * identity
    tangents = jnp.stack([variance * kernel, variance * scaled * scaled * jnp.exp(-scaled), identity]) + noise
    return jnp.concatenate([primal[None], tangents], axis=0)


def plant(entries, rng, least, top_value):
    index_at = [jax.random.randint(jax.random.fold_in(rng, axis), (), 0, length) for axis, length in enumerate(entries.shape)]
    longest = entries.shape.index(max(entries.shape))
    neighbour = index_at[:longest] + [(index_at[longest] + 1) % entries.shape[longest]] + index_at[longest + 1:]
    return entries.at[tuple(index_at)].set(least).at[tuple(neighbour)].set(top_value)


def bell_draw(own_key, extent, width, bound, kind=jnp.bfloat16):
    result = jax.random.normal(own_key, extent, jnp.float32) * width
    return jnp.minimum(jnp.maximum(result, -bound), bound).astype(kind)


def setup_inputs(seed: int = 0) -> dict:
    keys = jax.random.split(jax.random.key(seed), 10)
    diag = draw_diag(jax.random.fold_in(keys[9], 71), 0)
    panel_rows = draw_panel_rows(jax.random.fold_in(keys[9], 71), 0)
    panel_cols = draw_panel_cols(jax.random.fold_in(keys[9], 71), 0)
    trailing = draw_trailing(jax.random.fold_in(keys[9], 71), 0)
    sketch = bell_draw(keys[4], (RMAX, NB), 1.0, 6.0, jnp.float32)
    panel_rank = plant(jax.random.randint(keys[5], (TROWS,), RMAX // 4, RMAX + 1), jax.random.fold_in(keys[5], 1), RMAX // 4, RMAX).astype(jnp.int32)
    col_rank = plant(jax.random.randint(keys[6], (TCOLS,), RMAX // 4, RMAX + 1), jax.random.fold_in(keys[6], 1), RMAX // 4, RMAX).astype(jnp.int32)
    tile_rank = plant(jax.random.randint(keys[7], (TROWS, TCOLS), RMAX // 2, RMAX + 1), jax.random.fold_in(keys[7], 1), RMAX // 2, RMAX).astype(jnp.int32)
    keep_rank = plant(jax.random.randint(keys[8], (TROWS, TCOLS), RMAX // 8, RMAX // 2 + 1), jax.random.fold_in(keys[8], 1), RMAX // 8, (RMAX // 2 + 1) - 1).astype(jnp.int32)
    return {"diag": diag, "panel_rows": panel_rows, "panel_cols": panel_cols, "trailing": trailing, "sketch": sketch, "panel_rank": panel_rank, "col_rank": col_rank, "tile_rank": tile_rank, "keep_rank": keep_rank}


HIGHEST_PRECISION = lax.Precision.HIGHEST

def highest_accuracy(left, right):
    return jnp.dot(left.astype(jnp.float32), right.astype(jnp.float32), precision=HIGHEST_PRECISION, preferred_element_type=jnp.float32)

def rank_mask(rank_values, rank_count):
    return (jnp.arange(rank_count, dtype=jnp.int32) < rank_values[..., None]).astype(jnp.float32)

def inverse_apply(lower_factor, rank_rows):
    half_solved = jax.scipy.linalg.solve_triangular(lower_factor, rank_rows.T, lower=True)
    full_solved = jax.scipy.linalg.solve_triangular(lower_factor, half_solved, lower=True, trans=1)
    return full_solved.T

def sketch_apply(active_sketch, previous_left_factor, previous_right_factor, u_row, mix_in, u_col):
    return highest_accuracy(highest_accuracy(active_sketch, previous_right_factor.T), previous_left_factor) - highest_accuracy(highest_accuracy(highest_accuracy(active_sketch, u_col.T), mix_in.T), u_row)

def basis_apply(row_basis_matrix, previous_left_factor, previous_right_factor, u_row, mix_in, u_col):
    return highest_accuracy(highest_accuracy(row_basis_matrix, previous_left_factor.T), previous_right_factor) - highest_accuracy(highest_accuracy(highest_accuracy(row_basis_matrix, u_row.T), mix_in), u_col)

def compress_all(previous_left_factor, previous_right_factor, u_row, mix_in, u_col, du_old, dv_old, du_row, dmix_in, du_col, active_sketch, live_mask):
    sketched = sketch_apply(active_sketch, previous_left_factor, previous_right_factor, u_row, mix_in, u_col)
    gram_matrix = highest_accuracy(sketched, sketched.T) + jnp.diag(1.0 - live_mask)
    factor = jnp.linalg.cholesky(gram_matrix)
    row_basis_matrix = jax.scipy.linalg.solve_triangular(factor, sketched, lower=True)
    coefficients = basis_apply(row_basis_matrix, previous_left_factor, previous_right_factor, u_row, mix_in, u_col)
    up_scale = math.sqrt(previous_left_factor.shape[1])
    down_scale = math.sqrt(previous_left_factor.shape[0])

    def tangent_direction(previous_left_derivative, previous_right_derivative, row_left_derivative, mixing_derivative, column_left_derivative):
        sketch_derivative = highest_accuracy(highest_accuracy(active_sketch, previous_right_derivative.T), previous_left_factor) + highest_accuracy(highest_accuracy(active_sketch, previous_right_factor.T), previous_left_derivative)
        sketch_derivative = sketch_derivative - highest_accuracy(highest_accuracy(highest_accuracy(active_sketch, column_left_derivative.T), mix_in.T), u_row)
        sketch_derivative = sketch_derivative - highest_accuracy(highest_accuracy(highest_accuracy(active_sketch, u_col.T), mixing_derivative.T), u_row)
        sketch_derivative = sketch_derivative - highest_accuracy(highest_accuracy(highest_accuracy(active_sketch, u_col.T), mix_in.T), row_left_derivative)
        d_gram = highest_accuracy(sketch_derivative, sketched.T) + highest_accuracy(sketched, sketch_derivative.T)
        inner = jax.scipy.linalg.solve_triangular(factor, d_gram, lower=True)
        middle = jax.scipy.linalg.solve_triangular(factor, inner.T, lower=True)
        lower_part = jnp.tril(middle) - 0.5 * jnp.diag(jnp.diagonal(middle))
        d_factor = highest_accuracy(factor, lower_part)
        d_basis = jax.scipy.linalg.solve_triangular(factor, sketch_derivative - highest_accuracy(d_factor, row_basis_matrix), lower=True)
        coefficient_derivative = basis_apply(d_basis, previous_left_factor, previous_right_factor, u_row, mix_in, u_col)
        coefficient_derivative = coefficient_derivative + highest_accuracy(highest_accuracy(row_basis_matrix, previous_left_derivative.T), previous_right_factor) + highest_accuracy(highest_accuracy(row_basis_matrix, previous_left_factor.T), previous_right_derivative)
        coefficient_derivative = coefficient_derivative - highest_accuracy(highest_accuracy(highest_accuracy(row_basis_matrix, row_left_derivative.T), mix_in), u_col)
        coefficient_derivative = coefficient_derivative - highest_accuracy(highest_accuracy(highest_accuracy(row_basis_matrix, u_row.T), mixing_derivative), u_col)
        coefficient_derivative = coefficient_derivative - highest_accuracy(highest_accuracy(highest_accuracy(row_basis_matrix, u_row.T), mix_in), column_left_derivative)
        return (d_basis * up_scale, coefficient_derivative / down_scale)
    tangent_basis, tangent_coeff = jax.vmap(tangent_direction)(du_old, dv_old, du_row, dmix_in, du_col)
    return (row_basis_matrix * up_scale, coefficients / down_scale, tangent_basis, tangent_coeff)

def update_tile(row_tile, row_solved, col_tile, col_solved, col_products, old_tile, tile_mask, keep_mask, sketch):
    old_tile = old_tile * tile_mask[None, :, None]
    mixing = highest_accuracy(row_tile[4], col_solved.T)
    tangent_mix = jnp.stack([highest_accuracy(row_tile[5 + direction], col_solved.T) + highest_accuracy(row_solved, col_tile[5 + direction].T) - highest_accuracy(row_solved, col_products[direction].T) for direction in range(3)])
    active_sketch = sketch * keep_mask[:, None]
    basis_out, coeff_out, tangent_basis, tangent_coeff = compress_all(old_tile[0], old_tile[4], row_tile[0], mixing, col_tile[0], old_tile[1:4], old_tile[5:8], row_tile[1:4], tangent_mix, col_tile[1:4], active_sketch, keep_mask)
    return jnp.concatenate([basis_out[None], tangent_basis, coeff_out[None], tangent_coeff], axis=0)

def reference(diag, panel_rows, panel_cols, trailing, sketch, panel_rank, col_rank, tile_rank, keep_rank):
    lower_factor = jnp.linalg.cholesky(diag[0])
    rows_kept = panel_rows * rank_mask(panel_rank, RMAX)[:, None, :, None]
    cols_kept = panel_cols * rank_mask(col_rank, RMAX)[:, None, :, None]
    row_solved = inverse_apply(lower_factor, rows_kept[:, 4].reshape(-1, NB)).reshape(TROWS, RMAX, NB)
    col_solved = inverse_apply(lower_factor, cols_kept[:, 4].reshape(-1, NB)).reshape(TCOLS, RMAX, NB)
    col_products = jnp.einsum('caj,tij->ctai', col_solved, diag[1:], precision=HIGHEST_PRECISION)
    tile_live = rank_mask(tile_rank, RMAX)
    keep_live = rank_mask(keep_rank, RMAX)

    def one_row(row_items):
        row_tile, row_z, old_row, live_row, keep_row = row_items

        def one_tile(col_tile, col_z, col_prod, old_tile, tile_mask, keep_mask):
            return update_tile(row_tile, row_z, col_tile, col_z, col_prod, old_tile, tile_mask, keep_mask, sketch)
        return jax.vmap(one_tile)(cols_kept, col_solved, col_products, old_row, live_row, keep_row)
    return lax.map(one_row, (rows_kept, row_solved, trailing, tile_live, keep_live))
```

```python
import functools
import math

import jax
import jax.numpy as jnp
from jax import lax
from jax.experimental import pallas as pl
from jax.experimental.pallas import tpu as pltpu
from jax.sharding import PartitionSpec as P

HI = lax.Precision.HIGHEST
BLOCK = 128
NPIV = 8
LIVE = 32
F32 = jnp.float32


def nn(x, y):
    return lax.dot_general(
        x, y, (((1,), (0,)), ((), ())), precision=HI, preferred_element_type=F32
    )


def nt(x, y):
    return lax.dot_general(
        x, y, (((1,), (1,)), ((), ())), precision=HI, preferred_element_type=F32
    )


def total(terms):
    terms = list(terms)
    while len(terms) > 1:
        terms = [
            terms[i] + terms[i + 1] if i + 1 < len(terms) else terms[i]
            for i in range(0, len(terms), 2)
        ]
    return terms[0]


def small_inverse(m):
    n = len(m)
    if n == 1:
        return [[1.0 / m[0][0]]]
    if n == 2:
        r = 1.0 / (m[0][0] * m[1][1] - m[0][1] * m[0][1])
        return [[m[1][1] * r, -m[0][1] * r], [-m[0][1] * r, m[0][0] * r]]
    h = n // 2
    e = small_inverse([row[:h] for row in m[:h]])
    b = [row[h:] for row in m[:h]]
    x = [[total(e[i][k] * b[k][j] for k in range(h)) for j in range(h)] for i in range(h)]
    s = [[None] * h for _ in range(h)]
    for i in range(h):
        for j in range(i, h):
            s[i][j] = m[h + i][h + j] - total(b[k][i] * x[k][j] for k in range(h))
            s[j][i] = s[i][j]
    g = small_inverse(s)
    o = [[-total(x[i][k] * g[k][j] for k in range(h)) for j in range(h)] for i in range(h)]
    t = [[None] * h for _ in range(h)]
    for i in range(h):
        for j in range(i, h):
            t[i][j] = e[i][j] - total(o[i][k] * x[j][k] for k in range(h))
            t[j][i] = t[i][j]
    return [t[i] + o[i] for i in range(h)] + [[o[j][i] for j in range(h)] + g[i] for i in range(h)]


def block_inverse(d):
    n = d.shape[0]
    lane = lax.broadcasted_iota(jnp.int32, (n, n), 1)
    sub = lax.broadcasted_iota(jnp.int32, (n, n), 0)
    lane8 = lax.broadcasted_iota(jnp.int32, (8, n), 1)
    for j in range(0, n, NPIV):
        m = [[None] * NPIV for _ in range(NPIV)]
        for r in range(NPIV):
            for c in range(r, NPIV):
                m[r][c] = jnp.broadcast_to(d[j + r : j + r + 1, j + c : j + c + 1], (8, n))
                m[c][r] = m[r][c]
        cols = [jnp.broadcast_to(d[:, j + q : j + q + 1], (n, n)) for q in range(NPIV)]
        p = small_inverse(m)
        own = (lane8 >= j) & (lane8 < j + NPIV)
        rows = [
            jnp.where(own, (lane8 == j + q).astype(F32), jnp.broadcast_to(d[j + q : j + q + 1, :], (8, n)))
            for q in range(NPIV)
        ]
        new = [total(p[q][k] * rows[k] for k in range(NPIV)) for q in range(NPIV)]
        new = [jnp.concatenate([t] * (n // 8), axis=0) for t in new]
        out = jnp.where((lane >= j) & (lane < j + NPIV), 0.0, d)
        for q in range(NPIV):
            out = out - cols[q] * new[q]
        for q in range(NPIV):
            out = jnp.where(sub == j + q, new[q], out)
        d = out
    return d


def invert_kernel(a_ref, o_ref, c_ref):
    size = a_ref.shape[0]
    o_ref[...] = a_ref[...]

    def step(k, carry):
        off = pl.multiple_of(k * BLOCK, BLOCK)
        pivot = block_inverse(o_ref[pl.ds(off, BLOCK), pl.ds(off, BLOCK)])
        c_ref[...] = o_ref[:, pl.ds(off, BLOCK)]
        o_ref[pl.ds(off, BLOCK), :] = nn(pivot, o_ref[pl.ds(off, BLOCK), :])
        o_ref[pl.ds(off, BLOCK), pl.ds(off, BLOCK)] = pivot
        pivot_rows = o_ref[pl.ds(off, BLOCK), :]
        for q in range(size // BLOCK):
            rows = slice(q * BLOCK, (q + 1) * BLOCK)

            @pl.when(k != q)
            def _():
                o_ref[rows, pl.ds(off, BLOCK)] = jnp.zeros((BLOCK, BLOCK), F32)
                o_ref[rows, :] = o_ref[rows, :] - nn(c_ref[rows, :], pivot_rows)

        return carry

    lax.fori_loop(0, size // BLOCK, step, 0)


def column_kernel(v_ref, inv_ref, diag_ref, z_ref, f_ref):
    z = nn(v_ref[0, 4], inv_ref[...])
    z_ref[...] = z
    f_ref[...] = jnp.concatenate([nt(diag_ref[1 + t], z) for t in range(3)], axis=1)


def panel_rows_of(ref, comp):
    return jnp.concatenate([ref[piece, 0, comp] for piece in range(ref.shape[0])], axis=1)


def root_inverse(g):
    n, nb = LIVE, 4
    lane = lax.broadcasted_iota(jnp.int32, (n, 128), 1)
    sub = lax.broadcasted_iota(jnp.int32, (n, 128), 0)
    e = jnp.concatenate([g, jnp.zeros((n, 128 - n), F32)], axis=1) + (lane == sub + n).astype(F32)
    for j in range(0, n, nb):
        m = [[None] * nb for _ in range(nb)]
        for r in range(nb):
            for c in range(r, nb):
                m[r][c] = jnp.broadcast_to(e[j + r : j + r + 1, j + c : j + c + 1], (8, 128))
        cols = [jnp.broadcast_to(e[:, j + q : j + q + 1], (n, 128)) for q in range(nb)]
        rows = [jnp.broadcast_to(e[j + q : j + q + 1, :], (8, 128)) for q in range(nb)]
        rec = []
        for q in range(nb):
            rec.append(1.0 / m[q][q])
            low = {r: m[q][r] * rec[q] for r in range(q + 1, nb)}
            for r in range(q + 1, nb):
                for c in range(r, nb):
                    m[r][c] = m[r][c] - low[r] * m[q][c]
                rows[r] = rows[r] - low[r] * rows[q]
                cols[r] = cols[r] - jnp.concatenate([low[r]] * (n // 8), axis=0) * cols[q]
        rows_n = [jnp.concatenate([t] * (n // 8), axis=0) for t in rows]
        out = e
        for q in range(nb):
            out = out - (cols[q] * jnp.concatenate([rec[q]] * (n // 8), axis=0)) * rows_n[q]
        out = jnp.where(sub >= j + nb, out, e)
        for q in range(nb):
            out = jnp.where(sub == j + q, rows_n[q], out)
        e = out
    d = jnp.sum(jnp.where(lane == sub, e, 0.0), axis=1, keepdims=True)
    return e[:, n : 2 * n] * (1.0 / jnp.sqrt(d))


def prepare_kernel(
    prank_ref, crank_ref, trank_ref, krank_ref,
    rows_ref, cols_ref, tr_ref, s_ref, inv_ref, zc_ref,
    zp_ref, w_ref, h_ref, k_ref, ri_ref, q_ref,
):
    tile = pl.program_id(0)
    r = s_ref.shape[0]
    zc = zc_ref[...]
    zp = nn(panel_rows_of(rows_ref, 4), inv_ref[...])
    zp_ref[0] = zp
    keep_p = lax.broadcasted_iota(jnp.int32, (r, r), 0) < prank_ref[tile]
    keep_c = lax.broadcasted_iota(jnp.int32, (r, r), 1) < crank_ref[0]
    keep = keep_p & keep_c
    w0 = jnp.where(keep, nt(panel_rows_of(rows_ref, 4), zc), 0.0)
    w_ref[0, 0] = w0
    for t in range(3):
        w_ref[0, 1 + t] = nt(panel_rows_of(rows_ref, 5 + t), zc) + nt(zp, cols_ref[0, 5 + t])
    live = (lax.broadcasted_iota(jnp.int32, (LIVE, s_ref.shape[1]), 0) < krank_ref[tile, 0]).astype(F32)
    s = s_ref[0:LIVE, :] * live
    keep_t = lax.broadcasted_iota(jnp.int32, (LIVE, r), 1) < trank_ref[tile, 0]
    for t in range(4):
        h_ref[0, t] = jnp.where(keep_t, nt(s, tr_ref[0, 0, 4 + t]), 0.0)
        k_ref[0, t] = nt(s, cols_ref[0, t])
    left = jnp.concatenate([h_ref[0, 0], -nt(k_ref[0, 0], w0)], axis=1)
    up = jnp.concatenate([tr_ref[0, 0, 0], panel_rows_of(rows_ref, 0)], axis=0)
    y = nn(left, up)
    sub = lax.broadcasted_iota(jnp.int32, (LIVE, LIVE), 0)
    lane = lax.broadcasted_iota(jnp.int32, (LIVE, LIVE), 1)
    g = nt(y, y) + ((sub == lane) & (sub >= krank_ref[tile, 0])).astype(F32)
    ri = root_inverse(g)
    ri_ref[0] = ri
    q_ref[0] = nn(ri, y)


def finish_kernel(
    prank_ref, crank_ref, trank_ref,
    rows_ref, cols_ref, tr_ref, f_ref, zp_ref, w_ref, h_ref, k_ref, ri_ref, q_ref,
    o_ref,
):
    tile = pl.program_id(0)
    r = h_ref.shape[3]
    width = q_ref.shape[2]
    keep_p = lax.broadcasted_iota(jnp.int32, (r, r), 0) < prank_ref[tile]
    keep_c = lax.broadcasted_iota(jnp.int32, (r, r), 1) < crank_ref[0]
    keep = keep_p & keep_c
    keep_t = lax.broadcasted_iota(jnp.int32, (LIVE, r), 1) < trank_ref[tile, 0]
    zf = nn(zp_ref[0], f_ref[...])
    w0 = w_ref[0, 0]
    dw = [jnp.where(keep, w_ref[0, 1 + t] - zf[:, t * r : (t + 1) * r], 0.0) for t in range(3)]
    ri = ri_ref[0]
    q = q_ref[0]
    h = [h_ref[0, t] for t in range(4)]
    k = [k_ref[0, t] for t in range(4)]
    left0 = nn(ri, jnp.concatenate([h[0], -nt(k[0], w0)], axis=1))
    left = [
        nn(ri, jnp.concatenate([h[1 + t], -(nt(k[1 + t], w0) + nt(k[0], dw[t]))], axis=1))
        for t in range(3)
    ]
    ups = [jnp.concatenate([tr_ref[0, 0, t], panel_rows_of(rows_ref, t)], axis=0) for t in range(4)]
    e = nn(jnp.concatenate(left, axis=0), ups[0])
    e = e + jnp.concatenate([nn(left0, ups[1 + t]) for t in range(3)], axis=0)
    m = nt(e, q)
    sub = lax.broadcasted_iota(jnp.int32, (LIVE, LIVE), 0)
    lane = lax.broadcasted_iota(jnp.int32, (LIVE, LIVE), 1)
    phi = []
    for t in range(3):
        mt = m[t * LIVE : (t + 1) * LIVE, :]
        mid = mt + mt.T
        phi.append(jnp.where(sub > lane, mid, jnp.where(sub == lane, 0.5 * mid, 0.0)))
    dq = e - nn(jnp.concatenate(phi, axis=0), q)
    qs = jnp.concatenate([q, dq], axis=0)
    js = nt(qs, ups[0])
    extra = [nt(q, ups[1 + t]) for t in range(3)]
    j0 = js[0:LIVE]
    j0u, j0p = jnp.where(keep_t, j0[:, :r], 0.0), j0[:, r:]
    n0 = jnp.concatenate([j0u, -nn(j0p, w0)], axis=1)
    ns = [n0]
    for t in range(3):
        jt = js[(1 + t) * LIVE : (2 + t) * LIVE] + extra[t]
        ns.append(
            jnp.concatenate(
                [jnp.where(keep_t, jt[:, :r], 0.0), -(nn(jt[:, r:], w0) + nn(j0p, dw[t]))], axis=1
            )
        )
    vs = [jnp.concatenate([tr_ref[0, 0, 4 + t], cols_ref[0, t]], axis=0) for t in range(4)]
    b = nn(jnp.concatenate(ns, axis=0), vs[0])
    up_scale = math.sqrt(width)
    down_scale = 1.0 / math.sqrt(r)
    zero = jnp.zeros((r - LIVE, width), F32)
    for t in range(4):
        o_ref[0, 0, t, 0:LIVE, :] = qs[t * LIVE : (t + 1) * LIVE] * up_scale
        bt = b[t * LIVE : (t + 1) * LIVE]
        if t:
            bt = bt + nn(n0, vs[t])
        o_ref[0, 0, 4 + t, 0:LIVE, :] = bt * down_scale
        o_ref[0, 0, t, LIVE:r, :] = zero
        o_ref[0, 0, 4 + t, LIVE:r, :] = zero


def whole(shape):
    return pl.BlockSpec(shape, lambda i: (0,) * len(shape))


def tiled(shape):
    return pl.BlockSpec(shape, lambda i: (i,) + (0,) * (len(shape) - 1))


def params():
    return pltpu.CompilerParams(vmem_limit_bytes=56 << 20)


def cost(flops, nbytes):
    return pl.CostEstimate(flops=int(flops), bytes_accessed=int(nbytes), transcendentals=0)


def on_device(
    diag, panel_rows, panel_cols, trailing, sketch, panel_rank, col_rank, tile_rank, keep_rank
):
    rank, width = sketch.shape
    tiles = trailing.shape[0]
    pieces = lax.axis_size("col")
    a = lax.all_gather(diag[0], "row", axis=0, tiled=True)
    a, panel_rows, panel_cols = lax.optimization_barrier((a, panel_rows, panel_cols))
    cols = lax.all_gather(panel_cols, "row", axis=2, tiled=True)
    rows = lax.all_gather(panel_rows, "col", axis=0, tiled=False)
    inverse = pl.pallas_call(
        invert_kernel,
        out_shape=jax.ShapeDtypeStruct((width, width), F32),
        scratch_shapes=[pltpu.VMEM((width, BLOCK), F32)],
        compiler_params=params(),
        cost_estimate=cost(60e9, 8 << 20),
        name="invert",
    )(a)
    zc, f = pl.pallas_call(
        column_kernel,
        out_shape=(
            jax.ShapeDtypeStruct((rank, width), F32),
            jax.ShapeDtypeStruct((diag.shape[1], 3 * rank), F32),
        ),
        compiler_params=params(),
        cost_estimate=cost(2e9, 6 << 20),
        name="columns",
    )(cols, inverse, diag)
    f_all = lax.all_gather(f, "row", axis=0, tiled=True)
    smem = pl.BlockSpec(memory_space=pltpu.SMEM)
    rows_spec = pl.BlockSpec((pieces, 1) + rows.shape[2:], lambda i: (0, i, 0, 0, 0))
    tr_spec = tiled((1,) + trailing.shape[1:])
    mids = dict(
        zp=(tiles, rank, width),
        w=(tiles, 4, rank, rank),
        h=(tiles, 4, LIVE, rank),
        k=(tiles, 4, LIVE, rank),
        ri=(tiles, LIVE, LIVE),
        q=(tiles, LIVE, width),
    )
    mid_specs = [tiled((1,) + s[1:]) for s in mids.values()]
    mid = pl.pallas_call(
        prepare_kernel,
        grid=(tiles,),
        in_specs=[smem] * 4
        + [rows_spec, whole(cols.shape), tr_spec, whole(sketch.shape), whole(inverse.shape), whole(zc.shape)],
        out_specs=mid_specs,
        out_shape=[jax.ShapeDtypeStruct(s, F32) for s in mids.values()],
        compiler_params=params(),
        cost_estimate=cost(10e9, 20 << 20),
        name="prepare",
    )(panel_rank, col_rank, tile_rank, keep_rank, rows, cols, trailing, sketch, inverse, zc)
    return pl.pallas_call(
        finish_kernel,
        grid=(tiles,),
        in_specs=[smem] * 3
        + [rows_spec, whole(cols.shape), tr_spec, whole(f_all.shape)]
        + mid_specs,
        out_specs=tr_spec,
        out_shape=jax.ShapeDtypeStruct(trailing.shape, F32),
        compiler_params=params(),
        cost_estimate=cost(10e9, 20 << 20),
        name="finish",
    )(panel_rank, col_rank, tile_rank, rows, cols, trailing, f_all, *mid)


def solution(mesh):
    in_specs = (
        P(None, "row", None),
        P("row", None, None, "col"),
        P("col", None, "row", None),
        P("row", "col", None, None, None),
        P(),
        P("row"),
        P("col"),
        P("row", "col"),
        P("row", "col"),
    )
    out_specs = P("row", "col", None, None, None)
    return jax.shard_map(
        on_device, mesh=mesh, in_specs=in_specs, out_specs=out_specs, check_vma=False
    )
```

```python
import functools
import math

import jax
import jax.numpy as jnp
from jax import lax
from jax.experimental import pallas as pl
from jax.experimental.pallas import tpu as pltpu
from jax.sharding import PartitionSpec as P

HI = lax.Precision.HIGHEST
BLOCK = 128
NPIV = 8
LIVE = 32
F32 = jnp.float32
BF16 = jnp.bfloat16
MESH = pl.DeviceIdType.MESH
SIDE = 4
SENDS = 4 * SIDE + 2 * SIDE + SIDE * SIDE - SIDE + 2 + 2 + 2


def nn(x, y):
    return lax.dot_general(
        x, y, (((1,), (0,)), ((), ())), precision=HI, preferred_element_type=F32
    )


def nt(x, y):
    return lax.dot_general(
        x, y, (((1,), (1,)), ((), ())), precision=HI, preferred_element_type=F32
    )


def total(terms):
    terms = list(terms)
    while len(terms) > 1:
        terms = [
            terms[i] + terms[i + 1] if i + 1 < len(terms) else terms[i]
            for i in range(0, len(terms), 2)
        ]
    return terms[0]


def small_inverse(m):
    n = len(m)
    if n == 1:
        return [[1.0 / m[0][0]]]
    if n == 2:
        r = 1.0 / (m[0][0] * m[1][1] - m[0][1] * m[0][1])
        return [[m[1][1] * r, -m[0][1] * r], [-m[0][1] * r, m[0][0] * r]]
    h = n // 2
    e = small_inverse([row[:h] for row in m[:h]])
    b = [row[h:] for row in m[:h]]
    x = [[total(e[i][k] * b[k][j] for k in range(h)) for j in range(h)] for i in range(h)]
    s = [[None] * h for _ in range(h)]
    for i in range(h):
        for j in range(i, h):
            s[i][j] = m[h + i][h + j] - total(b[k][i] * x[k][j] for k in range(h))
            s[j][i] = s[i][j]
    g = small_inverse(s)
    o = [[-total(x[i][k] * g[k][j] for k in range(h)) for j in range(h)] for i in range(h)]
    t = [[None] * h for _ in range(h)]
    for i in range(h):
        for j in range(i, h):
            t[i][j] = e[i][j] - total(o[i][k] * x[j][k] for k in range(h))
            t[j][i] = t[i][j]
    return [t[i] + o[i] for i in range(h)] + [[o[j][i] for j in range(h)] + g[i] for i in range(h)]


def split3(x):
    a = x.astype(BF16)
    r = x - a.astype(F32)
    b = r.astype(BF16)
    return a, b, (r - b.astype(F32)).astype(BF16)


def left6(parts):
    a, b, c = parts
    return jnp.concatenate([a, b, a, b, a, c], axis=1)


def right6(parts):
    a, b, c = parts
    return jnp.concatenate([a, a, b, b, c, a], axis=0)


def mm(x, y):
    return lax.dot_general(x, y, (((1,), (0,)), ((), ())), preferred_element_type=F32)


def pivot_steps(d):
    n = d.shape[0]
    lane = lax.broadcasted_iota(jnp.int32, (n, n), 1)
    sub = lax.broadcasted_iota(jnp.int32, (n, n), 0)
    lane8 = lax.broadcasted_iota(jnp.int32, (8, n), 1)
    for j in range(0, n, NPIV):
        m = [[None] * NPIV for _ in range(NPIV)]
        for r in range(NPIV):
            for c in range(r, NPIV):
                m[r][c] = jnp.broadcast_to(d[j + r : j + r + 1, j + c : j + c + 1], (8, n))
                m[c][r] = m[r][c]
        cols = [jnp.broadcast_to(d[:, j + q : j + q + 1], (n, n)) for q in range(NPIV)]
        p = small_inverse(m)
        own = (lane8 >= j) & (lane8 < j + NPIV)
        rows = [
            jnp.where(own, (lane8 == j + q).astype(F32), jnp.broadcast_to(d[j + q : j + q + 1, :], (8, n)))
            for q in range(NPIV)
        ]
        new = [total(p[q][k] * rows[k] for k in range(NPIV)) for q in range(NPIV)]
        new = [jnp.concatenate([t] * (n // 8), axis=0) for t in new]
        out = jnp.where((lane >= j) & (lane < j + NPIV), 0.0, d)
        for q in range(NPIV):
            out = out - cols[q] * new[q]
        for q in range(NPIV):
            out = jnp.where(sub == j + q, new[q], out)
        d = out
        yield d


def invert_kernel(g_ref, o_ref, p_ref, l_ref, r_ref):
    size = o_ref.shape[0]
    blocks = size // BLOCK
    share = size // g_ref.shape[0]
    for i in range(g_ref.shape[0]):
        o_ref[i * share : (i + 1) * share, :] = g_ref[i, 0:share, :]
    d = None
    for d in pivot_steps(o_ref[0:BLOCK, 0:BLOCK]):
        pass
    p_ref[...] = d

    def step(k, last):
        off = pl.multiple_of(k * BLOCK, BLOCK)
        here = pl.ds(off, BLOCK)
        p = p_ref[...]
        p6 = left6(split3(p))
        for q, part in enumerate(split3(o_ref[:, here])):
            l_ref[:, q * BLOCK : (q + 1) * BLOCK] = part

        def left_of(row):
            return left6([l_ref[pl.ds(row, BLOCK), q * BLOCK : (q + 1) * BLOCK] for q in range(3)])

        steps, found = iter(()), None
        if not last:
            nxt = pl.multiple_of((k + 1) * BLOCK, BLOCK)
            rn = mm(p6, right6(split3(o_ref[here, pl.ds(nxt, BLOCK)])))
            steps = pivot_steps(
                o_ref[pl.ds(nxt, BLOCK), pl.ds(nxt, BLOCK)] - mm(left_of(nxt), right6(split3(rn)))
            )
        o_ref[here, here] = jnp.zeros((BLOCK, BLOCK), F32)
        for h in range(2):
            cs = slice(h * size // 2, (h + 1) * size // 2)
            o_ref[here, cs] = mm(p6, right6(split3(o_ref[here, cs])))
        o_ref[here, here] = p
        for q, part in enumerate(split3(o_ref[here, :])):
            r_ref[q * BLOCK : (q + 1) * BLOCK, :] = part
        for q in range(1, blocks):
            row = pl.multiple_of(lax.rem(k + q, blocks) * BLOCK, BLOCK)
            o_ref[pl.ds(row, BLOCK), here] = jnp.zeros((BLOCK, BLOCK), F32)
            left = left_of(row)
            for h in range(2):
                cs = slice(h * size // 2, (h + 1) * size // 2)
                right = right6([r_ref[q3 * BLOCK : (q3 + 1) * BLOCK, cs] for q3 in range(3)])
                o_ref[pl.ds(row, BLOCK), cs] = o_ref[pl.ds(row, BLOCK), cs] - mm(left, right)
                found = next(steps, found)
        for found in steps:
            pass
        if not last:
            p_ref[...] = found

    def body(k, carry):
        step(k, False)
        return carry

    lax.fori_loop(0, blocks - 1, body, 0)
    step(blocks - 1, True)


def gather_kernel(x_ref, o_ref, stage_ref, local_sem, send_sem, recv_sem, pair_sem):
    row = lax.axis_index("row")
    col = lax.axis_index("col")
    core = lax.rem(row, 2)
    x0 = lax.rem(row // 2, SIDE)
    y0 = row // (2 * SIDE)
    half = x_ref.shape[0] // 2

    def device(i1, i2, c=None):
        c = core if c is None else c
        dx = i1 * (1 - core) + i2 * core
        dy = i1 * core + i2 * (1 - core)
        return (lax.rem(y0 + dy + SIDE, SIDE) * SIDE + lax.rem(x0 + dx + SIDE, SIDE)) * 2 + c

    peers = {
        "a+": device(1, 0),
        "a-": device(-1, 0),
        "b+": device(0, 1),
        "b-": device(0, -1),
        "pair": device(0, 0, 1 - core),
    }
    shift = {"a+": (1, 0), "a-": (-1, 0), "b+": (0, 1), "b-": (0, -1)}
    barrier = pltpu.get_barrier_semaphore()
    for to in peers.values():
        pl.semaphore_signal(barrier, inc=1, device_id=(to, col), device_id_type=MESH)
    pl.semaphore_wait(barrier, len(peers))

    mine = pltpu.make_async_copy(x_ref, stage_ref, local_sem.at[0])
    mine.start()
    sent = []

    def part(ref, h):
        return ref if h is None else ref.at[pl.ds(h * half, half)]

    def send(i1, i2, to, h=None):
        owner = device(i1, i2)
        source = x_ref if (i1, i2) == (0, 0) else o_ref.at[owner]
        if to == "pair":
            sem = pair_sem.at[i1 % SIDE, i2 % SIDE]
        else:
            s1, s2 = shift[to]
            sem = recv_sem.at[(i1 - s1) % SIDE, (i2 - s2) % SIDE, h or 0]
        copy = pltpu.make_async_remote_copy(
            src_ref=part(source, h),
            dst_ref=part(o_ref.at[owner], h),
            send_sem=send_sem.at[len(sent)],
            recv_sem=sem,
            device_id=(peers[to], col),
            device_id_type=MESH,
        )
        copy.start()
        sent.append(copy)

    def arrive(i1, i2, h=None, pair=False):
        owner = device(i1, i2)
        sem = pair_sem.at[i1 % SIDE, i2 % SIDE] if pair else recv_sem.at[i1 % SIDE, i2 % SIDE, h or 0]
        dst = part(o_ref.at[owner], h)
        pltpu.make_async_remote_copy(
            src_ref=dst,
            dst_ref=dst,
            send_sem=send_sem.at[0],
            recv_sem=sem,
            device_id=(peers["pair"], col),
            device_id_type=MESH,
        ).wait_recv()

    def spread(i1):
        send(i1, 0, "b+")
        send(i1, 0, "b-")
        send(i1, 0, "pair")

    send(0, 0, "a+")
    send(0, 0, "a-")
    spread(0)
    mine.wait()
    keep = pltpu.make_async_copy(stage_ref, o_ref.at[row], local_sem.at[1])
    keep.start()
    arrive(-1, 0)
    send(-1, 0, "a+", 0)
    spread(-1)
    arrive(1, 0)
    send(1, 0, "a-", 1)
    spread(1)
    arrive(2, 0, 0)
    arrive(2, 0, 1)
    spread(2)
    order = (0, -1, 1, 2)
    for i1 in order:
        arrive(i1, -1)
        send(i1, -1, "b+", 0)
        send(i1, -1, "pair")
        arrive(i1, 1)
        send(i1, 1, "b-", 1)
        send(i1, 1, "pair")
    for i1 in order:
        arrive(i1, 2, 0)
        arrive(i1, 2, 1)
        send(i1, 2, "pair")
    for i1 in range(SIDE):
        for i2 in range(SIDE):
            arrive_pair(o_ref, device, pair_sem, send_sem, i1, i2, core, peers["pair"], col)
    for copy in sent:
        copy.wait_send()
    keep.wait()


def arrive_pair(o_ref, device, pair_sem, send_sem, i1, i2, core, pair, col):
    owner = device(i2, i1, 1 - core)
    pltpu.make_async_remote_copy(
        src_ref=o_ref.at[owner],
        dst_ref=o_ref.at[owner],
        send_sem=send_sem.at[0],
        recv_sem=pair_sem.at[i1, i2],
        device_id=(pair, col),
        device_id_type=MESH,
    ).wait_recv()


def gather(block, collective_id):
    devices = lax.axis_size("row")
    return pl.pallas_call(
        gather_kernel,
        out_shape=jax.ShapeDtypeStruct((devices,) + block.shape, F32),
        in_specs=[pl.BlockSpec(memory_space=pl.ANY)],
        out_specs=pl.BlockSpec(memory_space=pl.ANY),
        scratch_shapes=[
            pltpu.VMEM(block.shape, F32),
            pltpu.SemaphoreType.DMA((2,)),
            pltpu.SemaphoreType.DMA((SENDS,)),
            pltpu.SemaphoreType.DMA((SIDE, SIDE, 2)),
            pltpu.SemaphoreType.DMA((SIDE, SIDE)),
        ],
        compiler_params=pltpu.CompilerParams(collective_id=collective_id, has_side_effects=True),
        cost_estimate=cost(0, 12 << 20),
        name="gather",
    )(block)


def column_kernel(g_ref, inv_ref, diag_ref, z_ref, f_ref, c_ref):
    devices, extent, width = g_ref.shape
    share = width // devices
    for i in range(devices):
        for j in range((extent - share) // 8):
            c_ref[:, i * ((extent - share) // 8) + j, :] = g_ref[i, share + 8 * j : share + 8 * (j + 1), :]
    z = nn(c_ref[4], inv_ref[...])
    z_ref[...] = z
    f_ref[...] = jnp.concatenate([nt(diag_ref[1 + t], z) for t in range(3)], axis=1)


def panel_rows_of(ref, comp):
    return jnp.concatenate([ref[piece, 0, comp] for piece in range(ref.shape[0])], axis=1)


def root_inverse(g):
    n, nb = LIVE, 4
    lane = lax.broadcasted_iota(jnp.int32, (n, 128), 1)
    sub = lax.broadcasted_iota(jnp.int32, (n, 128), 0)
    e = jnp.concatenate([g, jnp.zeros((n, 128 - n), F32)], axis=1) + (lane == sub + n).astype(F32)
    for j in range(0, n, nb):
        m = [[None] * nb for _ in range(nb)]
        for r in range(nb):
            for c in range(r, nb):
                m[r][c] = jnp.broadcast_to(e[j + r : j + r + 1, j + c : j + c + 1], (8, 128))
        cols = [jnp.broadcast_to(e[:, j + q : j + q + 1], (n, 128)) for q in range(nb)]
        rows = [jnp.broadcast_to(e[j + q : j + q + 1, :], (8, 128)) for q in range(nb)]
        rec = []
        for q in range(nb):
            rec.append(1.0 / m[q][q])
            low = {r: m[q][r] * rec[q] for r in range(q + 1, nb)}
            for r in range(q + 1, nb):
                for c in range(r, nb):
                    m[r][c] = m[r][c] - low[r] * m[q][c]
                rows[r] = rows[r] - low[r] * rows[q]
                cols[r] = cols[r] - jnp.concatenate([low[r]] * (n // 8), axis=0) * cols[q]
        rows_n = [jnp.concatenate([t] * (n // 8), axis=0) for t in rows]
        out = e
        for q in range(nb):
            out = out - (cols[q] * jnp.concatenate([rec[q]] * (n // 8), axis=0)) * rows_n[q]
        out = jnp.where(sub >= j + nb, out, e)
        for q in range(nb):
            out = jnp.where(sub == j + q, rows_n[q], out)
        e = out
    d = jnp.sum(jnp.where(lane == sub, e, 0.0), axis=1, keepdims=True)
    return e[:, n : 2 * n] * (1.0 / jnp.sqrt(d))


def prepare_kernel(
    prank_ref, crank_ref, trank_ref, krank_ref,
    rows_ref, cols_ref, tr_ref, s_ref, inv_ref, zc_ref,
    zp_ref, w_ref, h_ref, k_ref, ri_ref, q_ref,
):
    tile = pl.program_id(0)
    r = s_ref.shape[0]
    zc = zc_ref[...]
    zp = nn(panel_rows_of(rows_ref, 4), inv_ref[...])
    zp_ref[0] = zp
    keep_p = lax.broadcasted_iota(jnp.int32, (r, r), 0) < prank_ref[tile]
    keep_c = lax.broadcasted_iota(jnp.int32, (r, r), 1) < crank_ref[0]
    keep = keep_p & keep_c
    w0 = jnp.where(keep, nt(panel_rows_of(rows_ref, 4), zc), 0.0)
    w_ref[0, 0] = w0
    for t in range(3):
        w_ref[0, 1 + t] = nt(panel_rows_of(rows_ref, 5 + t), zc) + nt(zp, cols_ref[5 + t])
    live = (lax.broadcasted_iota(jnp.int32, (LIVE, s_ref.shape[1]), 0) < krank_ref[tile, 0]).astype(F32)
    s = s_ref[0:LIVE, :] * live
    keep_t = lax.broadcasted_iota(jnp.int32, (LIVE, r), 1) < trank_ref[tile, 0]
    for t in range(4):
        h_ref[0, t] = jnp.where(keep_t, nt(s, tr_ref[0, 0, 4 + t]), 0.0)
        k_ref[0, t] = nt(s, cols_ref[t])
    left = jnp.concatenate([h_ref[0, 0], -nt(k_ref[0, 0], w0)], axis=1)
    up = jnp.concatenate([tr_ref[0, 0, 0], panel_rows_of(rows_ref, 0)], axis=0)
    y = nn(left, up)
    sub = lax.broadcasted_iota(jnp.int32, (LIVE, LIVE), 0)
    lane = lax.broadcasted_iota(jnp.int32, (LIVE, LIVE), 1)
    g = nt(y, y) + ((sub == lane) & (sub >= krank_ref[tile, 0])).astype(F32)
    ri = root_inverse(g)
    ri_ref[0] = ri
    q_ref[0] = nn(ri, y)


def finish_kernel(
    prank_ref, crank_ref, trank_ref,
    rows_ref, cols_ref, tr_ref, f_ref, zp_ref, w_ref, h_ref, k_ref, ri_ref, q_ref,
    o_ref,
):
    tile = pl.program_id(0)
    r = h_ref.shape[3]
    width = q_ref.shape[2]
    keep_p = lax.broadcasted_iota(jnp.int32, (r, r), 0) < prank_ref[tile]
    keep_c = lax.broadcasted_iota(jnp.int32, (r, r), 1) < crank_ref[0]
    keep = keep_p & keep_c
    keep_t = lax.broadcasted_iota(jnp.int32, (LIVE, r), 1) < trank_ref[tile, 0]
    zf = nn(zp_ref[0], f_ref[...])
    w0 = w_ref[0, 0]
    dw = [jnp.where(keep, w_ref[0, 1 + t] - zf[:, t * r : (t + 1) * r], 0.0) for t in range(3)]
    ri = ri_ref[0]
    q = q_ref[0]
    h = [h_ref[0, t] for t in range(4)]
    k = [k_ref[0, t] for t in range(4)]
    left0 = nn(ri, jnp.concatenate([h[0], -nt(k[0], w0)], axis=1))
    left = [
        nn(ri, jnp.concatenate([h[1 + t], -(nt(k[1 + t], w0) + nt(k[0], dw[t]))], axis=1))
        for t in range(3)
    ]
    ups = [jnp.concatenate([tr_ref[0, 0, t], panel_rows_of(rows_ref, t)], axis=0) for t in range(4)]
    e = nn(jnp.concatenate(left, axis=0), ups[0])
    e = e + jnp.concatenate([nn(left0, ups[1 + t]) for t in range(3)], axis=0)
    m = nt(e, q)
    sub = lax.broadcasted_iota(jnp.int32, (LIVE, LIVE), 0)
    lane = lax.broadcasted_iota(jnp.int32, (LIVE, LIVE), 1)
    phi = []
    for t in range(3):
        mt = m[t * LIVE : (t + 1) * LIVE, :]
        mid = mt + mt.T
        phi.append(jnp.where(sub > lane, mid, jnp.where(sub == lane, 0.5 * mid, 0.0)))
    dq = e - nn(jnp.concatenate(phi, axis=0), q)
    qs = jnp.concatenate([q, dq], axis=0)
    js = nt(qs, ups[0])
    extra = [nt(q, ups[1 + t]) for t in range(3)]
    j0 = js[0:LIVE]
    j0u, j0p = jnp.where(keep_t, j0[:, :r], 0.0), j0[:, r:]
    n0 = jnp.concatenate([j0u, -nn(j0p, w0)], axis=1)
    ns = [n0]
    for t in range(3):
        jt = js[(1 + t) * LIVE : (2 + t) * LIVE] + extra[t]
        ns.append(
            jnp.concatenate(
                [jnp.where(keep_t, jt[:, :r], 0.0), -(nn(jt[:, r:], w0) + nn(j0p, dw[t]))], axis=1
            )
        )
    vs = [jnp.concatenate([tr_ref[0, 0, 4 + t], cols_ref[t]], axis=0) for t in range(4)]
    b = nn(jnp.concatenate(ns, axis=0), vs[0])
    up_scale = math.sqrt(width)
    down_scale = 1.0 / math.sqrt(r)
    zero = jnp.zeros((r - LIVE, width), F32)
    for t in range(4):
        o_ref[0, 0, t, 0:LIVE, :] = qs[t * LIVE : (t + 1) * LIVE] * up_scale
        bt = b[t * LIVE : (t + 1) * LIVE]
        if t:
            bt = bt + nn(n0, vs[t])
        o_ref[0, 0, 4 + t, 0:LIVE, :] = bt * down_scale
        o_ref[0, 0, t, LIVE:r, :] = zero
        o_ref[0, 0, 4 + t, LIVE:r, :] = zero


def whole(shape):
    return pl.BlockSpec(shape, lambda i: (0,) * len(shape))


def tiled(shape):
    return pl.BlockSpec(shape, lambda i: (i,) + (0,) * (len(shape) - 1))


def params():
    return pltpu.CompilerParams(vmem_limit_bytes=56 << 20)


def cost(flops, nbytes):
    return pl.CostEstimate(flops=int(flops), bytes_accessed=int(nbytes), transcendentals=0)


def on_device(
    diag, panel_rows, panel_cols, trailing, sketch, panel_rank, col_rank, tile_rank, keep_rank
):
    rank, width = sketch.shape
    tiles = trailing.shape[0]
    pieces = lax.axis_size("col")
    rows = lax.all_gather(panel_rows, "col", axis=0, tiled=False)
    own_cols = panel_cols[0].transpose(1, 0, 2).reshape(-1, width)
    gathered = gather(jnp.concatenate([diag[0], own_cols], axis=0), 1)
    inverse = pl.pallas_call(
        invert_kernel,
        out_shape=jax.ShapeDtypeStruct((width, width), F32),
        scratch_shapes=[
            pltpu.VMEM((BLOCK, BLOCK), F32),
            pltpu.VMEM((width, 3 * BLOCK), BF16),
            pltpu.VMEM((3 * BLOCK, width), BF16),
        ],
        compiler_params=params(),
        cost_estimate=cost(60e9, 8 << 20),
        name="invert",
    )(gathered)
    zc, f, cols = pl.pallas_call(
        column_kernel,
        out_shape=(
            jax.ShapeDtypeStruct((rank, width), F32),
            jax.ShapeDtypeStruct((diag.shape[1], 3 * rank), F32),
            jax.ShapeDtypeStruct((panel_cols.shape[1], rank, width), F32),
        ),
        compiler_params=params(),
        cost_estimate=cost(2e9, 6 << 20),
        name="columns",
    )(gathered, inverse, diag)
    f_all = gather(f, 2).reshape(width, 3 * rank)
    smem = pl.BlockSpec(memory_space=pltpu.SMEM)
    rows_spec = pl.BlockSpec((pieces, 1) + rows.shape[2:], lambda i: (0, i, 0, 0, 0))
    tr_spec = tiled((1,) + trailing.shape[1:])
    mids = dict(
        zp=(tiles, rank, width),
        w=(tiles, 4, rank, rank),
        h=(tiles, 4, LIVE, rank),
        k=(tiles, 4, LIVE, rank),
        ri=(tiles, LIVE, LIVE),
        q=(tiles, LIVE, width),
    )
    mid_specs = [tiled((1,) + s[1:]) for s in mids.values()]
    mid = pl.pallas_call(
        prepare_kernel,
        grid=(tiles,),
        in_specs=[smem] * 4
        + [rows_spec, whole(cols.shape), tr_spec, whole(sketch.shape), whole(inverse.shape), whole(zc.shape)],
        out_specs=mid_specs,
        out_shape=[jax.ShapeDtypeStruct(s, F32) for s in mids.values()],
        compiler_params=params(),
        cost_estimate=cost(10e9, 20 << 20),
        name="prepare",
    )(panel_rank, col_rank, tile_rank, keep_rank, rows, cols, trailing, sketch, inverse, zc)
    return pl.pallas_call(
        finish_kernel,
        grid=(tiles,),
        in_specs=[smem] * 3
        + [rows_spec, whole(cols.shape), tr_spec, whole(f_all.shape)]
        + mid_specs,
        out_specs=tr_spec,
        out_shape=jax.ShapeDtypeStruct(trailing.shape, F32),
        compiler_params=params(),
        cost_estimate=cost(10e9, 20 << 20),
        name="finish",
    )(panel_rank, col_rank, tile_rank, rows, cols, trailing, f_all, *mid)


def solution(mesh):
    in_specs = (
        P(None, "row", None),
        P("row", None, None, "col"),
        P("col", None, "row", None),
        P("row", "col", None, None, None),
        P(),
        P("row"),
        P("col"),
        P("row", "col"),
        P("row", "col"),
    )
    out_specs = P("row", "col", None, None, None)
    return jax.shard_map(
        on_device, mesh=mesh, in_specs=in_specs, out_specs=out_specs, check_vma=False
    )
```

```python
import functools
import math

import jax
import jax.numpy as jnp
from jax import lax
from jax.experimental import pallas as pl
from jax.experimental.pallas import tpu as pltpu
from jax.sharding import PartitionSpec as P

HI = lax.Precision.HIGHEST
BLOCK = 128
NPIV = 8
LIVE = 32
F32 = jnp.float32
BF16 = jnp.bfloat16
MESH = pl.DeviceIdType.MESH
SIDE = 4
SENDS = 4 * SIDE + 2 * SIDE + SIDE * SIDE - SIDE + 2 + 2 + 2


def nn(x, y):
    return lax.dot_general(
        x, y, (((1,), (0,)), ((), ())), precision=HI, preferred_element_type=F32
    )


def nt(x, y):
    return lax.dot_general(
        x, y, (((1,), (1,)), ((), ())), precision=HI, preferred_element_type=F32
    )


def total(terms):
    terms = list(terms)
    while len(terms) > 1:
        terms = [
            terms[i] + terms[i + 1] if i + 1 < len(terms) else terms[i]
            for i in range(0, len(terms), 2)
        ]
    return terms[0]


def small_inverse(m):
    n = len(m)
    if n == 1:
        return [[1.0 / m[0][0]]]
    if n == 2:
        r = 1.0 / (m[0][0] * m[1][1] - m[0][1] * m[0][1])
        return [[m[1][1] * r, -m[0][1] * r], [-m[0][1] * r, m[0][0] * r]]
    h = n // 2
    e = small_inverse([row[:h] for row in m[:h]])
    b = [row[h:] for row in m[:h]]
    x = [[total(e[i][k] * b[k][j] for k in range(h)) for j in range(h)] for i in range(h)]
    s = [[None] * h for _ in range(h)]
    for i in range(h):
        for j in range(i, h):
            s[i][j] = m[h + i][h + j] - total(b[k][i] * x[k][j] for k in range(h))
            s[j][i] = s[i][j]
    g = small_inverse(s)
    o = [[-total(x[i][k] * g[k][j] for k in range(h)) for j in range(h)] for i in range(h)]
    t = [[None] * h for _ in range(h)]
    for i in range(h):
        for j in range(i, h):
            t[i][j] = e[i][j] - total(o[i][k] * x[j][k] for k in range(h))
            t[j][i] = t[i][j]
    return [t[i] + o[i] for i in range(h)] + [[o[j][i] for j in range(h)] + g[i] for i in range(h)]


def split3(x):
    a = x.astype(BF16)
    r = x - a.astype(F32)
    b = r.astype(BF16)
    return a, b, (r - b.astype(F32)).astype(BF16)


def left6(parts):
    a, b, c = parts
    return jnp.concatenate([a, b, a, b, a, c], axis=1)


def right6(parts):
    a, b, c = parts
    return jnp.concatenate([a, a, b, b, c, a], axis=0)


def mm(x, y):
    return lax.dot_general(x, y, (((1,), (0,)), ((), ())), preferred_element_type=F32)


def split2(x):
    a = x.astype(BF16)
    return a, (x - a.astype(F32)).astype(BF16)


def nn2(x, y):
    m = x.shape[0]
    a, b = split2(x)
    left = jnp.concatenate([jnp.concatenate([a, a], axis=1), jnp.concatenate([b, b], axis=1)], axis=0)
    r = mm(left, jnp.concatenate(split2(y), axis=0))
    return r[:m] + r[m:]


def nn3(x, y):
    m = x.shape[0]
    a, b, c = split3(x)
    ya, yb, yc = split3(y)
    r = mm(jnp.concatenate([a, b, c], axis=0), ya)
    q = mm(jnp.concatenate([a, b], axis=0), yb)
    return ((r[2 * m :] + mm(a, yc)) + q[m:]) + (r[m : 2 * m] + q[:m]) + r[:m]


def nt2(x, y):
    m, n = x.shape[0], y.shape[0]
    r = lax.dot_general(
        jnp.concatenate(split2(x), axis=0),
        jnp.concatenate(split2(y), axis=0),
        (((1,), (1,)), ((), ())),
        preferred_element_type=F32,
    )
    r = r[:m] + r[m:]
    return r[:, :n] + r[:, n:]


def pivot_steps(d):
    n = d.shape[0]
    lane = lax.broadcasted_iota(jnp.int32, (n, n), 1)
    sub = lax.broadcasted_iota(jnp.int32, (n, n), 0)
    lane8 = lax.broadcasted_iota(jnp.int32, (8, n), 1)
    for j in range(0, n, NPIV):
        m = [[None] * NPIV for _ in range(NPIV)]
        for r in range(NPIV):
            for c in range(r, NPIV):
                m[r][c] = jnp.broadcast_to(d[j + r : j + r + 1, j + c : j + c + 1], (8, n))
                m[c][r] = m[r][c]
        cols = [jnp.broadcast_to(d[:, j + q : j + q + 1], (n, n)) for q in range(NPIV)]
        p = small_inverse(m)
        own = (lane8 >= j) & (lane8 < j + NPIV)
        rows = [
            jnp.where(own, (lane8 == j + q).astype(F32), jnp.broadcast_to(d[j + q : j + q + 1, :], (8, n)))
            for q in range(NPIV)
        ]
        new = [total(p[q][k] * rows[k] for k in range(NPIV)) for q in range(NPIV)]
        new = [jnp.concatenate([t] * (n // 8), axis=0) for t in new]
        out = jnp.where((lane >= j) & (lane < j + NPIV), 0.0, d)
        for q in range(NPIV):
            out = out - cols[q] * new[q]
        for q in range(NPIV):
            out = jnp.where(sub == j + q, new[q], out)
        d = out
        yield d


def invert_kernel(g_ref, o_ref, p_ref, l_ref, r_ref):
    size = o_ref.shape[0]
    blocks = size // BLOCK
    share = size // g_ref.shape[0]
    for i in range(g_ref.shape[0]):
        o_ref[i * share : (i + 1) * share, :] = g_ref[i, 0:share, :]
    d = None
    for d in pivot_steps(o_ref[0:BLOCK, 0:BLOCK]):
        pass
    p_ref[...] = d

    def step(k, last):
        off = pl.multiple_of(k * BLOCK, BLOCK)
        here = pl.ds(off, BLOCK)
        p = p_ref[...]
        p6 = left6(split3(p))
        for q, part in enumerate(split3(o_ref[:, here])):
            l_ref[:, q * BLOCK : (q + 1) * BLOCK] = part

        def left_of(row):
            return left6([l_ref[pl.ds(row, BLOCK), q * BLOCK : (q + 1) * BLOCK] for q in range(3)])

        steps, found = iter(()), None
        if not last:
            nxt = pl.multiple_of((k + 1) * BLOCK, BLOCK)
            rn = mm(p6, right6(split3(o_ref[here, pl.ds(nxt, BLOCK)])))
            steps = pivot_steps(
                o_ref[pl.ds(nxt, BLOCK), pl.ds(nxt, BLOCK)] - mm(left_of(nxt), right6(split3(rn)))
            )
        o_ref[here, here] = jnp.zeros((BLOCK, BLOCK), F32)
        for h in range(2):
            cs = slice(h * size // 2, (h + 1) * size // 2)
            o_ref[here, cs] = mm(p6, right6(split3(o_ref[here, cs])))
        o_ref[here, here] = p
        for q, part in enumerate(split3(o_ref[here, :])):
            r_ref[q * BLOCK : (q + 1) * BLOCK, :] = part
        for q in range(1, blocks):
            row = pl.multiple_of(lax.rem(k + q, blocks) * BLOCK, BLOCK)
            o_ref[pl.ds(row, BLOCK), here] = jnp.zeros((BLOCK, BLOCK), F32)
            left = left_of(row)
            for h in range(2):
                cs = slice(h * size // 2, (h + 1) * size // 2)
                right = right6([r_ref[q3 * BLOCK : (q3 + 1) * BLOCK, cs] for q3 in range(3)])
                o_ref[pl.ds(row, BLOCK), cs] = o_ref[pl.ds(row, BLOCK), cs] - mm(left, right)
                found = next(steps, found)
        for found in steps:
            pass
        if not last:
            p_ref[...] = found

    def body(k, carry):
        step(k, False)
        return carry

    lax.fori_loop(0, blocks - 1, body, 0)
    step(blocks - 1, True)


def gather_kernel(x_ref, o_ref, stage_ref, local_sem, send_sem, recv_sem, pair_sem):
    row = lax.axis_index("row")
    col = lax.axis_index("col")
    core = lax.rem(row, 2)
    x0 = lax.rem(row // 2, SIDE)
    y0 = row // (2 * SIDE)
    half = x_ref.shape[0] // 2

    def device(i1, i2, c=None):
        c = core if c is None else c
        dx = i1 * (1 - core) + i2 * core
        dy = i1 * core + i2 * (1 - core)
        return (lax.rem(y0 + dy + SIDE, SIDE) * SIDE + lax.rem(x0 + dx + SIDE, SIDE)) * 2 + c

    peers = {
        "a+": device(1, 0),
        "a-": device(-1, 0),
        "b+": device(0, 1),
        "b-": device(0, -1),
        "pair": device(0, 0, 1 - core),
    }
    shift = {"a+": (1, 0), "a-": (-1, 0), "b+": (0, 1), "b-": (0, -1)}
    barrier = pltpu.get_barrier_semaphore()
    for to in peers.values():
        pl.semaphore_signal(barrier, inc=1, device_id=(to, col), device_id_type=MESH)
    pl.semaphore_wait(barrier, len(peers))

    mine = pltpu.make_async_copy(x_ref, stage_ref, local_sem.at[0])
    mine.start()
    sent = []

    def part(ref, h):
        return ref if h is None else ref.at[pl.ds(h * half, half)]

    def send(i1, i2, to, h=None):
        owner = device(i1, i2)
        source = x_ref if (i1, i2) == (0, 0) else o_ref.at[owner]
        if to == "pair":
            sem = pair_sem.at[i1 % SIDE, i2 % SIDE]
        else:
            s1, s2 = shift[to]
            sem = recv_sem.at[(i1 - s1) % SIDE, (i2 - s2) % SIDE, h or 0]
        copy = pltpu.make_async_remote_copy(
            src_ref=part(source, h),
            dst_ref=part(o_ref.at[owner], h),
            send_sem=send_sem.at[len(sent)],
            recv_sem=sem,
            device_id=(peers[to], col),
            device_id_type=MESH,
        )
        copy.start()
        sent.append(copy)

    def arrive(i1, i2, h=None, pair=False):
        owner = device(i1, i2)
        sem = pair_sem.at[i1 % SIDE, i2 % SIDE] if pair else recv_sem.at[i1 % SIDE, i2 % SIDE, h or 0]
        dst = part(o_ref.at[owner], h)
        pltpu.make_async_remote_copy(
            src_ref=dst,
            dst_ref=dst,
            send_sem=send_sem.at[0],
            recv_sem=sem,
            device_id=(peers["pair"], col),
            device_id_type=MESH,
        ).wait_recv()

    def spread(i1):
        send(i1, 0, "b+")
        send(i1, 0, "b-")
        send(i1, 0, "pair")

    send(0, 0, "a+")
    send(0, 0, "a-")
    spread(0)
    mine.wait()
    keep = pltpu.make_async_copy(stage_ref, o_ref.at[row], local_sem.at[1])
    keep.start()
    arrive(-1, 0)
    send(-1, 0, "a+", 0)
    spread(-1)
    arrive(1, 0)
    send(1, 0, "a-", 1)
    spread(1)
    arrive(2, 0, 0)
    arrive(2, 0, 1)
    spread(2)
    order = (0, -1, 1, 2)
    for i1 in order:
        arrive(i1, -1)
        send(i1, -1, "b+", 0)
        send(i1, -1, "pair")
        arrive(i1, 1)
        send(i1, 1, "b-", 1)
        send(i1, 1, "pair")
    for i1 in order:
        arrive(i1, 2, 0)
        arrive(i1, 2, 1)
        send(i1, 2, "pair")
    for i1 in range(SIDE):
        for i2 in range(SIDE):
            arrive_pair(o_ref, device, pair_sem, send_sem, i1, i2, core, peers["pair"], col)
    for copy in sent:
        copy.wait_send()
    keep.wait()


def arrive_pair(o_ref, device, pair_sem, send_sem, i1, i2, core, pair, col):
    owner = device(i2, i1, 1 - core)
    pltpu.make_async_remote_copy(
        src_ref=o_ref.at[owner],
        dst_ref=o_ref.at[owner],
        send_sem=send_sem.at[0],
        recv_sem=pair_sem.at[i1, i2],
        device_id=(pair, col),
        device_id_type=MESH,
    ).wait_recv()


def gather(block, collective_id):
    devices = lax.axis_size("row")
    return pl.pallas_call(
        gather_kernel,
        out_shape=jax.ShapeDtypeStruct((devices,) + block.shape, F32),
        in_specs=[pl.BlockSpec(memory_space=pl.ANY)],
        out_specs=pl.BlockSpec(memory_space=pl.ANY),
        scratch_shapes=[
            pltpu.VMEM(block.shape, F32),
            pltpu.SemaphoreType.DMA((2,)),
            pltpu.SemaphoreType.DMA((SENDS,)),
            pltpu.SemaphoreType.DMA((SIDE, SIDE, 2)),
            pltpu.SemaphoreType.DMA((SIDE, SIDE)),
        ],
        compiler_params=pltpu.CompilerParams(collective_id=collective_id, has_side_effects=True),
        cost_estimate=cost(0, 12 << 20),
        name="gather",
    )(block)


def column_kernel(g_ref, rows_ref, inv_ref, diag_ref, zc_ref, zp_ref, f_ref, c_ref):
    devices, extent, width = g_ref.shape
    share = width // devices
    for i in range(devices):
        for j in range((extent - share) // 8):
            c_ref[:, i * ((extent - share) // 8) + j, :] = g_ref[i, share + 8 * j : share + 8 * (j + 1), :]
    tiles = rows_ref.shape[1]
    v = jnp.concatenate([c_ref[4]] + [panel_rows_of(rows_ref, t, 0) for t in range(tiles)], axis=0)
    z = nn3(v, inv_ref[...])
    r = zc_ref.shape[0]
    zc_ref[...] = z[:r]
    for t in range(tiles):
        zp_ref[t] = z[(1 + t) * r : (2 + t) * r]
    f = nt(diag_ref[1:4].reshape(3 * share, width), z[:r])
    f_ref[...] = jnp.concatenate([f[t * share : (t + 1) * share] for t in range(3)], axis=1)


def panel_rows_of(ref, tile, comp):
    return jnp.concatenate([ref[piece, tile, comp] for piece in range(ref.shape[0])], axis=1)


def root_inverse(g):
    n, nb = LIVE, 4
    lane = lax.broadcasted_iota(jnp.int32, (n, 128), 1)
    sub = lax.broadcasted_iota(jnp.int32, (n, 128), 0)
    e = jnp.concatenate([g, jnp.zeros((n, 128 - n), F32)], axis=1) + (lane == sub + n).astype(F32)
    for j in range(0, n, nb):
        m = [[None] * nb for _ in range(nb)]
        for r in range(nb):
            for c in range(r, nb):
                m[r][c] = jnp.broadcast_to(e[j + r : j + r + 1, j + c : j + c + 1], (8, 128))
        cols = [jnp.broadcast_to(e[:, j + q : j + q + 1], (n, 128)) for q in range(nb)]
        rows = [jnp.broadcast_to(e[j + q : j + q + 1, :], (8, 128)) for q in range(nb)]
        rec = []
        for q in range(nb):
            rec.append(1.0 / m[q][q])
            low = {r: m[q][r] * rec[q] for r in range(q + 1, nb)}
            for r in range(q + 1, nb):
                for c in range(r, nb):
                    m[r][c] = m[r][c] - low[r] * m[q][c]
                rows[r] = rows[r] - low[r] * rows[q]
                cols[r] = cols[r] - jnp.concatenate([low[r]] * (n // 8), axis=0) * cols[q]
        rows_n = [jnp.concatenate([t] * (n // 8), axis=0) for t in rows]
        out = e
        for q in range(nb):
            out = out - (cols[q] * jnp.concatenate([rec[q]] * (n // 8), axis=0)) * rows_n[q]
        out = jnp.where(sub >= j + nb, out, e)
        for q in range(nb):
            out = jnp.where(sub == j + q, rows_n[q], out)
        e = out
    d = jnp.sum(jnp.where(lane == sub, e, 0.0), axis=1, keepdims=True)
    return e[:, n : 2 * n] * (1.0 / jnp.sqrt(d))


def prepare_kernel(
    prank_ref, crank_ref, trank_ref, krank_ref,
    rows_hbm, cols_hbm, tr_hbm, s_ref, zc_ref, zp_ref, f_hbm,
    w_ref, h_ref, k_ref, ri_ref, q_ref,
    rows_ref, cols_ref, tr_ref, f_ref, load_sem, send_sem, recv_sem, give_sem, take_sem,
):
    row = lax.axis_index("row")
    col = lax.axis_index("col")
    devices = f_ref.shape[0]
    core = lax.rem(row, 2)
    pair = row + 1 - 2 * core
    chips = devices // 2
    tiles, r = zp_ref.shape[0], zp_ref.shape[1]
    width = s_ref.shape[1]
    others = [lax.rem(row + 2 * n, devices) for n in range(1, chips)]
    sources = [lax.rem(row - 2 * n + devices, devices) for n in range(1, chips)]
    barrier = pltpu.get_barrier_semaphore()
    for to in others + [pair]:
        pl.semaphore_signal(barrier, inc=1, device_id=(to, col), device_id_type=MESH)
    loads = [
        pltpu.make_async_copy(cols_hbm, cols_ref, load_sem.at[0]),
        pltpu.make_async_copy(tr_hbm, tr_ref, load_sem.at[1]),
        pltpu.make_async_copy(rows_hbm, rows_ref, load_sem.at[2]),
        pltpu.make_async_copy(f_hbm, f_ref.at[row], load_sem.at[3]),
    ]
    for copy in loads:
        copy.start()
    pl.semaphore_wait(barrier, chips)

    def remote(src, slot, to, ssem, rsem):
        return pltpu.make_async_remote_copy(
            src_ref=src, dst_ref=f_ref.at[slot], send_sem=ssem, recv_sem=rsem,
            device_id=(to, col), device_id_type=MESH,
        )

    sends = [remote(f_hbm, row, to, send_sem.at[n], recv_sem.at[n]) for n, to in enumerate(others)]
    for copy in sends:
        copy.start()
    gives = [remote(f_hbm, row, pair, give_sem.at[chips - 1], take_sem.at[chips - 1])]
    gives[0].start()

    loads[0].wait()
    loads[1].wait()
    s = s_ref[0:LIVE, :]
    big = [cols_ref[t] for t in range(4)]
    for i in range(tiles):
        big += [tr_ref[i, 0, 4 + t] for t in range(4)]
    hk = nt2(s, jnp.concatenate(big, axis=0))
    live = lax.broadcasted_iota(jnp.int32, (LIVE, 4 * r), 0)
    for i in range(tiles):
        k = jnp.where(live < krank_ref[i, 0], hk[:, 0 : 4 * r], 0.0)
        h = jnp.where(live < krank_ref[i, 0], hk[:, (1 + i) * 4 * r : (2 + i) * 4 * r], 0.0)
        keep_t = lax.broadcasted_iota(jnp.int32, (LIVE, r), 1) < trank_ref[i, 0]
        for t in range(4):
            h_ref[i, t] = jnp.where(keep_t, h[:, t * r : (t + 1) * r], 0.0)
            k_ref[i, t] = k[:, t * r : (t + 1) * r]
    loads[2].wait()
    zc = zc_ref[...]
    v = jnp.concatenate(
        [panel_rows_of(rows_ref, i, 4 + t) for i in range(tiles) for t in range(4)], axis=0
    )
    w_all = nt2(v, zc)
    sub = lax.broadcasted_iota(jnp.int32, (LIVE, LIVE), 0)
    lane = lax.broadcasted_iota(jnp.int32, (LIVE, LIVE), 1)
    keeps = []
    for i in range(tiles):
        keeps.append(
            (lax.broadcasted_iota(jnp.int32, (r, r), 0) < prank_ref[i])
            & (lax.broadcasted_iota(jnp.int32, (r, r), 1) < crank_ref[0])
        )
        w0 = jnp.where(keeps[i], w_all[4 * i * r : (4 * i + 1) * r], 0.0)
        w_ref[i, 0] = w0
        left = jnp.concatenate([h_ref[i, 0], -nt(k_ref[i, 0], w0)], axis=1)
        y = nn(left, jnp.concatenate([tr_ref[i, 0, 0], panel_rows_of(rows_ref, i, 0)], axis=0))
        g = nt(y, y) + ((sub == lane) & (sub >= krank_ref[i, 0])).astype(F32)
        ri = root_inverse(g)
        ri_ref[i] = ri
        q_ref[i] = nn(ri, y)
    zp = jnp.concatenate([zp_ref[i] for i in range(tiles)], axis=0)
    zv = nt2(zp, jnp.concatenate([cols_ref[5 + t] for t in range(3)], axis=0))

    for n, source in enumerate(sources):
        remote(f_hbm, source, pair, send_sem.at[n], recv_sem.at[n]).wait_recv()
        gives.append(remote(f_ref.at[source], source, pair, give_sem.at[n], take_sem.at[n]))
        gives[-1].start()
    for n in range(1, chips):
        slot = lax.rem(pair - 2 * n + devices, devices)
        remote(f_hbm, slot, pair, give_sem.at[n - 1], take_sem.at[n - 1]).wait_recv()
    remote(f_hbm, pair, pair, give_sem.at[chips - 1], take_sem.at[chips - 1]).wait_recv()
    loads[3].wait()
    zf = nn(zp, f_ref[...].reshape(width, f_ref.shape[2]))
    for i in range(tiles):
        for t in range(3):
            dw = w_all[(4 * i + 1 + t) * r : (4 * i + 2 + t) * r]
            part = zv[i * r : (i + 1) * r, t * r : (t + 1) * r] - zf[i * r : (i + 1) * r, t * r : (t + 1) * r]
            w_ref[i, 1 + t] = jnp.where(keeps[i], dw + part, 0.0)
    for copy in sends + gives:
        copy.wait_send()


def finish_kernel(
    trank_ref, rows_ref, cols_ref, tr_ref, w_ref, h_ref, k_ref, ri_ref, q_ref, o_ref
):
    tile = pl.program_id(0)
    r = h_ref.shape[3]
    width = q_ref.shape[2]
    keep_t = lax.broadcasted_iota(jnp.int32, (LIVE, r), 1) < trank_ref[tile, 0]
    w0 = w_ref[0, 0]
    dw = [w_ref[0, 1 + t] for t in range(3)]
    ri = ri_ref[0]
    q = q_ref[0]
    h = [h_ref[0, t] for t in range(4)]
    k = jnp.concatenate([k_ref[0, t] for t in range(4)], axis=0)
    kw = nt(k, w0)
    kd = nt(k_ref[0, 0], jnp.concatenate(dw, axis=0))
    left = [jnp.concatenate([h[0], -kw[0:LIVE]], axis=1)]
    for t in range(3):
        left.append(
            jnp.concatenate(
                [h[1 + t], -(kw[(1 + t) * LIVE : (2 + t) * LIVE] + kd[:, t * r : (t + 1) * r])], axis=1
            )
        )
    left = nn(ri, jnp.concatenate(left, axis=1))
    left0 = left[:, 0 : 2 * r]
    ups = [
        jnp.concatenate([tr_ref[0, 0, t], panel_rows_of(rows_ref, 0, t)], axis=0) for t in range(4)
    ]
    e = nn2(jnp.concatenate([left[:, 2 * r * t : 2 * r * (t + 1)] for t in (1, 2, 3)], axis=0), ups[0])
    e = e + jnp.concatenate([nn2(left0, ups[1 + t]) for t in range(3)], axis=0)
    m = nt2(e, q)
    sub = lax.broadcasted_iota(jnp.int32, (LIVE, LIVE), 0)
    lane = lax.broadcasted_iota(jnp.int32, (LIVE, LIVE), 1)
    phi = []
    for t in range(3):
        mt = m[t * LIVE : (t + 1) * LIVE, :]
        mid = mt + mt.T
        phi.append(jnp.where(sub > lane, mid, jnp.where(sub == lane, 0.5 * mid, 0.0)))
    dq = e - nn(jnp.concatenate(phi, axis=0), q)
    qs = jnp.concatenate([q, dq], axis=0)
    js = nt2(qs, ups[0])
    extra = nt2(q, jnp.concatenate(ups[1:], axis=0))
    js = [js[0:LIVE]] + [
        js[(1 + t) * LIVE : (2 + t) * LIVE] + extra[:, 2 * r * t : 2 * r * (t + 1)] for t in range(3)
    ]
    jw = nn(jnp.concatenate([j[:, r:] for j in js], axis=0), w0)
    jd = nn(js[0][:, r:], jnp.concatenate(dw, axis=1))
    ns = []
    for t in range(4):
        b = jw[t * LIVE : (t + 1) * LIVE]
        if t:
            b = b + jd[:, (t - 1) * r : t * r]
        ns.append(jnp.concatenate([jnp.where(keep_t, js[t][:, :r], 0.0), -b], axis=1))
    vs = [jnp.concatenate([tr_ref[0, 0, 4 + t], cols_ref[t]], axis=0) for t in range(4)]
    b = nn2(jnp.concatenate(ns, axis=0), vs[0])
    up_scale = math.sqrt(width)
    down_scale = 1.0 / math.sqrt(r)
    zero = jnp.zeros((r - LIVE, width), F32)
    for t in range(4):
        o_ref[0, 0, t, 0:LIVE, :] = qs[t * LIVE : (t + 1) * LIVE] * up_scale
        bt = b[t * LIVE : (t + 1) * LIVE]
        if t:
            bt = bt + nn2(ns[0], vs[t])
        o_ref[0, 0, 4 + t, 0:LIVE, :] = bt * down_scale
        o_ref[0, 0, t, LIVE:r, :] = zero
        o_ref[0, 0, 4 + t, LIVE:r, :] = zero


def whole(shape):
    return pl.BlockSpec(shape, lambda i: (0,) * len(shape))


def tiled(shape):
    return pl.BlockSpec(shape, lambda i: (i,) + (0,) * (len(shape) - 1))


def params():
    return pltpu.CompilerParams(vmem_limit_bytes=56 << 20)


def cost(flops, nbytes):
    return pl.CostEstimate(flops=int(flops), bytes_accessed=int(nbytes), transcendentals=0)


def on_device(
    diag, panel_rows, panel_cols, trailing, sketch, panel_rank, col_rank, tile_rank, keep_rank
):
    rank, width = sketch.shape
    tiles = trailing.shape[0]
    pieces = lax.axis_size("col")
    rows = lax.all_gather(panel_rows, "col", axis=0, tiled=False)
    own_cols = panel_cols[0].transpose(1, 0, 2).reshape(-1, width)
    gathered = gather(jnp.concatenate([diag[0], own_cols], axis=0), 1)
    inverse = pl.pallas_call(
        invert_kernel,
        out_shape=jax.ShapeDtypeStruct((width, width), F32),
        scratch_shapes=[
            pltpu.VMEM((BLOCK, BLOCK), F32),
            pltpu.VMEM((width, 3 * BLOCK), BF16),
            pltpu.VMEM((3 * BLOCK, width), BF16),
        ],
        compiler_params=params(),
        cost_estimate=cost(60e9, 8 << 20),
        name="invert",
    )(gathered)
    vmem = pl.BlockSpec(memory_space=pltpu.VMEM)
    hbm = pl.BlockSpec(memory_space=pl.ANY)
    smem = pl.BlockSpec(memory_space=pltpu.SMEM)
    v_spec = pl.BlockSpec(
        (pieces, tiles, 1) + rows.shape[3:], lambda i: (0, 0, 4, 0, 0)
    )
    outs = dict(
        zc=(rank, width),
        zp=(tiles, rank, width),
        f=(diag.shape[1], 3 * rank),
        cols=(panel_cols.shape[1], rank, width),
    )
    zc, zp, f, cols = pl.pallas_call(
        column_kernel,
        grid=(1,),
        in_specs=[whole(gathered.shape), v_spec, whole(inverse.shape), whole(diag.shape)],
        out_specs=[whole(v) for v in outs.values()],
        out_shape=[jax.ShapeDtypeStruct(v, F32) for v in outs.values()],
        compiler_params=params(),
        cost_estimate=cost(2e9, 6 << 20),
        name="columns",
    )(gathered, rows, inverse, diag)
    mids = dict(
        w=(tiles, 4, rank, rank),
        h=(tiles, 4, LIVE, rank),
        k=(tiles, 4, LIVE, rank),
        ri=(tiles, LIVE, LIVE),
        q=(tiles, LIVE, width),
    )
    devices = lax.axis_size("row")
    mid = pl.pallas_call(
        prepare_kernel,
        in_specs=[smem] * 4 + [hbm] * 3 + [vmem] * 3 + [hbm],
        out_specs=[vmem] * len(mids),
        out_shape=[jax.ShapeDtypeStruct(v, F32) for v in mids.values()],
        scratch_shapes=[
            pltpu.VMEM(rows.shape, F32),
            pltpu.VMEM(cols.shape, F32),
            pltpu.VMEM(trailing.shape, F32),
            pltpu.VMEM((devices,) + f.shape, F32),
            pltpu.SemaphoreType.DMA((4,)),
            pltpu.SemaphoreType.DMA((devices // 2 - 1,)),
            pltpu.SemaphoreType.DMA((devices // 2 - 1,)),
            pltpu.SemaphoreType.DMA((devices // 2,)),
            pltpu.SemaphoreType.DMA((devices // 2,)),
        ],
        compiler_params=pltpu.CompilerParams(
            vmem_limit_bytes=56 << 20, collective_id=2, has_side_effects=True
        ),
        cost_estimate=cost(10e9, 20 << 20),
        name="prepare",
    )(panel_rank, col_rank, tile_rank, keep_rank, rows, cols, trailing, sketch, zc, zp, f)
    tr_spec = tiled((1,) + trailing.shape[1:])
    return pl.pallas_call(
        finish_kernel,
        grid=(tiles,),
        in_specs=[
            smem,
            pl.BlockSpec((pieces, 1, 4) + rows.shape[3:], lambda i: (0, i, 0, 0, 0)),
            pl.BlockSpec((4,) + cols.shape[1:], lambda i: (0, 0, 0)),
            tr_spec,
        ]
        + [tiled((1,) + v[1:]) for v in mids.values()],
        out_specs=tr_spec,
        out_shape=jax.ShapeDtypeStruct(trailing.shape, F32),
        compiler_params=params(),
        cost_estimate=cost(10e9, 20 << 20),
        name="finish",
    )(tile_rank, rows, cols, trailing, *mid)


def solution(mesh):
    in_specs = (
        P(None, "row", None),
        P("row", None, None, "col"),
        P("col", None, "row", None),
        P("row", "col", None, None, None),
        P(),
        P("row"),
        P("col"),
        P("row", "col"),
        P("row", "col"),
    )
    out_specs = P("row", "col", None, None, None)
    return jax.shard_map(
        on_device, mesh=mesh, in_specs=in_specs, out_specs=out_specs, check_vma=False
    )
```

```python
import functools
import math

import jax
import jax.numpy as jnp
from jax import lax
from jax.experimental import pallas as pl
from jax.experimental.pallas import tpu as pltpu
from jax.sharding import PartitionSpec as P

HI = lax.Precision.HIGHEST
BLOCK = 128
NPIV = 8
LIVE = 32
F32 = jnp.float32
BF16 = jnp.bfloat16
MESH = pl.DeviceIdType.MESH
SIDE = 4
SENDS = 4 * SIDE + 2 * SIDE + SIDE * SIDE - SIDE + 2 + 2 + 2


def nn(x, y):
    return lax.dot_general(
        x, y, (((1,), (0,)), ((), ())), precision=HI, preferred_element_type=F32
    )


def nt(x, y):
    return lax.dot_general(
        x, y, (((1,), (1,)), ((), ())), precision=HI, preferred_element_type=F32
    )


def total(terms):
    terms = list(terms)
    while len(terms) > 1:
        terms = [
            terms[i] + terms[i + 1] if i + 1 < len(terms) else terms[i]
            for i in range(0, len(terms), 2)
        ]
    return terms[0]


def small_inverse(m):
    n = len(m)
    if n == 1:
        return [[1.0 / m[0][0]]]
    if n == 2:
        r = 1.0 / (m[0][0] * m[1][1] - m[0][1] * m[0][1])
        return [[m[1][1] * r, -m[0][1] * r], [-m[0][1] * r, m[0][0] * r]]
    h = n // 2
    e = small_inverse([row[:h] for row in m[:h]])
    b = [row[h:] for row in m[:h]]
    x = [[total(e[i][k] * b[k][j] for k in range(h)) for j in range(h)] for i in range(h)]
    s = [[None] * h for _ in range(h)]
    for i in range(h):
        for j in range(i, h):
            s[i][j] = m[h + i][h + j] - total(b[k][i] * x[k][j] for k in range(h))
            s[j][i] = s[i][j]
    g = small_inverse(s)
    o = [[-total(x[i][k] * g[k][j] for k in range(h)) for j in range(h)] for i in range(h)]
    t = [[None] * h for _ in range(h)]
    for i in range(h):
        for j in range(i, h):
            t[i][j] = e[i][j] - total(o[i][k] * x[j][k] for k in range(h))
            t[j][i] = t[i][j]
    return [t[i] + o[i] for i in range(h)] + [[o[j][i] for j in range(h)] + g[i] for i in range(h)]


def split3(x):
    a = x.astype(BF16)
    r = x - a.astype(F32)
    b = r.astype(BF16)
    return a, b, (r - b.astype(F32)).astype(BF16)


def left6(parts):
    a, b, c = parts
    return jnp.concatenate([a, b, a, b, a, c], axis=1)


def right6(parts):
    a, b, c = parts
    return jnp.concatenate([a, a, b, b, c, a], axis=0)


def mm(x, y):
    return lax.dot_general(x, y, (((1,), (0,)), ((), ())), preferred_element_type=F32)


def split2(x):
    a = x.astype(BF16)
    return a, (x - a.astype(F32)).astype(BF16)


def nn2(x, y):
    m = x.shape[0]
    a, b = split2(x)
    left = jnp.concatenate([jnp.concatenate([a, a], axis=1), jnp.concatenate([b, b], axis=1)], axis=0)
    r = mm(left, jnp.concatenate(split2(y), axis=0))
    return r[:m] + r[m:]


def nn3(x, y):
    m = x.shape[0]
    a, b, c = split3(x)
    ya, yb, yc = split3(y)
    r = mm(jnp.concatenate([a, b, c], axis=0), ya)
    q = mm(jnp.concatenate([a, b], axis=0), yb)
    return ((r[2 * m :] + mm(a, yc)) + q[m:]) + (r[m : 2 * m] + q[:m]) + r[:m]


def nt2(x, y):
    m, n = x.shape[0], y.shape[0]
    r = lax.dot_general(
        jnp.concatenate(split2(x), axis=0),
        jnp.concatenate(split2(y), axis=0),
        (((1,), (1,)), ((), ())),
        preferred_element_type=F32,
    )
    r = r[:m] + r[m:]
    return r[:, :n] + r[:, n:]


def pivot_steps(d):
    n, half = d.shape[0], NPIV // 2
    sub8 = lax.broadcasted_iota(jnp.int32, (8, n), 0)
    lane8 = lax.broadcasted_iota(jnp.int32, (8, n), 1)
    v = [d[8 * i : 8 * i + 8, :] for i in range(n // 8)]
    for g in range(n // 8):
        j = NPIV * g
        cols = [jnp.broadcast_to(v[g][:, j + q : j + q + 1], (8, n)) for q in range(NPIV)]
        m = [[None] * NPIV for _ in range(NPIV)]
        for r in range(NPIV):
            for c in range(r, NPIV):
                m[r][c] = jnp.broadcast_to(cols[c][r : r + 1, :], (8, n))
                m[c][r] = m[r][c]
        own = (lane8 >= j) & (lane8 < j + NPIV)
        rows = [
            jnp.where(own, (lane8 == j + q).astype(F32), jnp.broadcast_to(v[g][q : q + 1, :], (8, n)))
            for q in range(NPIV)
        ]
        span = range(half)
        e = small_inverse([row[:half] for row in m[:half]])
        b = [row[half:] for row in m[:half]]
        x = [[total(e[i][k] * b[k][q] for k in span) for q in span] for i in span]
        s = [[None] * half for _ in span]
        for i in span:
            for q in range(i, half):
                s[i][q] = m[half + i][half + q] - total(b[k][i] * x[k][q] for k in span)
                s[q][i] = s[i][q]
        f = small_inverse(s)
        top = [total(e[i][k] * rows[k] for k in span) for i in span]
        low = [rows[half + i] - total(b[k][i] * top[k] for k in span) for i in span]
        low = [total(f[i][k] * low[k] for k in span) for i in span]
        new = [top[i] - total(x[i][k] * low[k] for k in span) for i in span] + low
        out = [None] * len(v)
        first = (g + 1) % len(v)
        for i in [first] + [k for k in range(len(v)) if k != first]:
            if i == g:
                t = new[0]
                for q in range(1, NPIV):
                    t = jnp.where(sub8 == q, new[q], t)
            else:
                t = jnp.where(own, 0.0, v[i])
                for q in list(range(half, NPIV)) + list(range(half)):
                    t = t - jnp.broadcast_to(v[i][:, j + q : j + q + 1], (8, n)) * new[q]
            out[i] = t
        v = out
        yield jnp.concatenate(v, axis=0)


def invert_kernel(g_ref, o_ref, p_ref, l_ref, r_ref):
    size = o_ref.shape[0]
    blocks = size // BLOCK
    share = size // g_ref.shape[0]
    for i in range(g_ref.shape[0]):
        o_ref[i * share : (i + 1) * share, :] = g_ref[i, 0:share, :]
    d = None
    for d in pivot_steps(o_ref[0:BLOCK, 0:BLOCK]):
        pass
    p_ref[...] = d

    def step(k, last):
        off = pl.multiple_of(k * BLOCK, BLOCK)
        here = pl.ds(off, BLOCK)
        p = p_ref[...]
        p6 = left6(split3(p))
        for q, part in enumerate(split3(o_ref[:, here])):
            l_ref[:, q * BLOCK : (q + 1) * BLOCK] = part

        def left_of(row):
            return left6([l_ref[pl.ds(row, BLOCK), q * BLOCK : (q + 1) * BLOCK] for q in range(3)])

        steps, found = iter(()), None
        if not last:
            nxt = pl.multiple_of((k + 1) * BLOCK, BLOCK)
            rn = mm(p6, right6(split3(o_ref[here, pl.ds(nxt, BLOCK)])))
            steps = pivot_steps(
                o_ref[pl.ds(nxt, BLOCK), pl.ds(nxt, BLOCK)] - mm(left_of(nxt), right6(split3(rn)))
            )
        o_ref[here, here] = jnp.zeros((BLOCK, BLOCK), F32)
        for h in range(2):
            cs = slice(h * size // 2, (h + 1) * size // 2)
            o_ref[here, cs] = mm(p6, right6(split3(o_ref[here, cs])))
        o_ref[here, here] = p
        for q, part in enumerate(split3(o_ref[here, :])):
            r_ref[q * BLOCK : (q + 1) * BLOCK, :] = part
        for q in range(1, blocks):
            row = pl.multiple_of(lax.rem(k + q, blocks) * BLOCK, BLOCK)
            o_ref[pl.ds(row, BLOCK), here] = jnp.zeros((BLOCK, BLOCK), F32)
            left = left_of(row)
            for h in range(2):
                cs = slice(h * size // 2, (h + 1) * size // 2)
                right = right6([r_ref[q3 * BLOCK : (q3 + 1) * BLOCK, cs] for q3 in range(3)])
                o_ref[pl.ds(row, BLOCK), cs] = o_ref[pl.ds(row, BLOCK), cs] - mm(left, right)
                found = next(steps, found)
        for found in steps:
            pass
        if not last:
            p_ref[...] = found

    def body(k, carry):
        step(k, False)
        return carry

    lax.fori_loop(0, blocks - 1, body, 0)
    step(blocks - 1, True)


def gather_kernel(x_ref, o_ref, stage_ref, local_sem, send_sem, recv_sem, pair_sem):
    row = lax.axis_index("row")
    col = lax.axis_index("col")
    core = lax.rem(row, 2)
    x0 = lax.rem(row // 2, SIDE)
    y0 = row // (2 * SIDE)
    half = x_ref.shape[0] // 2

    def device(i1, i2, c=None):
        c = core if c is None else c
        dx = i1 * (1 - core) + i2 * core
        dy = i1 * core + i2 * (1 - core)
        return (lax.rem(y0 + dy + SIDE, SIDE) * SIDE + lax.rem(x0 + dx + SIDE, SIDE)) * 2 + c

    peers = {
        "a+": device(1, 0),
        "a-": device(-1, 0),
        "b+": device(0, 1),
        "b-": device(0, -1),
        "pair": device(0, 0, 1 - core),
    }
    shift = {"a+": (1, 0), "a-": (-1, 0), "b+": (0, 1), "b-": (0, -1)}
    barrier = pltpu.get_barrier_semaphore()
    for to in peers.values():
        pl.semaphore_signal(barrier, inc=1, device_id=(to, col), device_id_type=MESH)
    pl.semaphore_wait(barrier, len(peers))

    mine = pltpu.make_async_copy(x_ref, stage_ref, local_sem.at[0])
    mine.start()
    sent = []

    def part(ref, h):
        return ref if h is None else ref.at[pl.ds(h * half, half)]

    def send(i1, i2, to, h=None):
        owner = device(i1, i2)
        source = x_ref if (i1, i2) == (0, 0) else o_ref.at[owner]
        if to == "pair":
            sem = pair_sem.at[i1 % SIDE, i2 % SIDE]
        else:
            s1, s2 = shift[to]
            sem = recv_sem.at[(i1 - s1) % SIDE, (i2 - s2) % SIDE, h or 0]
        copy = pltpu.make_async_remote_copy(
            src_ref=part(source, h),
            dst_ref=part(o_ref.at[owner], h),
            send_sem=send_sem.at[len(sent)],
            recv_sem=sem,
            device_id=(peers[to], col),
            device_id_type=MESH,
        )
        copy.start()
        sent.append(copy)

    def arrive(i1, i2, h=None, pair=False):
        owner = device(i1, i2)
        sem = pair_sem.at[i1 % SIDE, i2 % SIDE] if pair else recv_sem.at[i1 % SIDE, i2 % SIDE, h or 0]
        dst = part(o_ref.at[owner], h)
        pltpu.make_async_remote_copy(
            src_ref=dst,
            dst_ref=dst,
            send_sem=send_sem.at[0],
            recv_sem=sem,
            device_id=(peers["pair"], col),
            device_id_type=MESH,
        ).wait_recv()

    def spread(i1):
        send(i1, 0, "b+")
        send(i1, 0, "b-")
        send(i1, 0, "pair")

    send(0, 0, "a+")
    send(0, 0, "a-")
    spread(0)
    mine.wait()
    keep = pltpu.make_async_copy(stage_ref, o_ref.at[row], local_sem.at[1])
    keep.start()
    arrive(-1, 0)
    send(-1, 0, "a+", 0)
    spread(-1)
    arrive(1, 0)
    send(1, 0, "a-", 1)
    spread(1)
    arrive(2, 0, 0)
    arrive(2, 0, 1)
    spread(2)
    order = (0, -1, 1, 2)
    for i1 in order:
        arrive(i1, -1)
        send(i1, -1, "b+", 0)
        send(i1, -1, "pair")
        arrive(i1, 1)
        send(i1, 1, "b-", 1)
        send(i1, 1, "pair")
    for i1 in order:
        arrive(i1, 2, 0)
        arrive(i1, 2, 1)
        send(i1, 2, "pair")
    for i1 in range(SIDE):
        for i2 in range(SIDE):
            arrive_pair(o_ref, device, pair_sem, send_sem, i1, i2, core, peers["pair"], col)
    for copy in sent:
        copy.wait_send()
    keep.wait()


def arrive_pair(o_ref, device, pair_sem, send_sem, i1, i2, core, pair, col):
    owner = device(i2, i1, 1 - core)
    pltpu.make_async_remote_copy(
        src_ref=o_ref.at[owner],
        dst_ref=o_ref.at[owner],
        send_sem=send_sem.at[0],
        recv_sem=pair_sem.at[i1, i2],
        device_id=(pair, col),
        device_id_type=MESH,
    ).wait_recv()


def gather(block, collective_id):
    devices = lax.axis_size("row")
    return pl.pallas_call(
        gather_kernel,
        out_shape=jax.ShapeDtypeStruct((devices,) + block.shape, F32),
        in_specs=[pl.BlockSpec(memory_space=pl.ANY)],
        out_specs=pl.BlockSpec(memory_space=pl.ANY),
        scratch_shapes=[
            pltpu.VMEM(block.shape, F32),
            pltpu.SemaphoreType.DMA((2,)),
            pltpu.SemaphoreType.DMA((SENDS,)),
            pltpu.SemaphoreType.DMA((SIDE, SIDE, 2)),
            pltpu.SemaphoreType.DMA((SIDE, SIDE)),
        ],
        compiler_params=pltpu.CompilerParams(collective_id=collective_id, has_side_effects=True),
        cost_estimate=cost(0, 12 << 20),
        name="gather",
    )(block)


def column_kernel(g_ref, rows_ref, inv_ref, diag_ref, zc_ref, zp_ref, f_ref, c_ref):
    devices, extent, width = g_ref.shape
    share = width // devices
    for i in range(devices):
        for j in range((extent - share) // 8):
            c_ref[:, i * ((extent - share) // 8) + j, :] = g_ref[i, share + 8 * j : share + 8 * (j + 1), :]
    tiles = rows_ref.shape[1]
    v = jnp.concatenate([c_ref[4]] + [panel_rows_of(rows_ref, t, 0) for t in range(tiles)], axis=0)
    z = nn3(v, inv_ref[...])
    r = zc_ref.shape[0]
    zc_ref[...] = z[:r]
    for t in range(tiles):
        zp_ref[t] = z[(1 + t) * r : (2 + t) * r]
    f = nt(diag_ref[1:4].reshape(3 * share, width), z[:r])
    f_ref[...] = jnp.concatenate([f[t * share : (t + 1) * share] for t in range(3)], axis=1)


def panel_rows_of(ref, tile, comp):
    return jnp.concatenate([ref[piece, tile, comp] for piece in range(ref.shape[0])], axis=1)


def root_inverse(g):
    n, nb = LIVE, 4
    lane = lax.broadcasted_iota(jnp.int32, (n, 128), 1)
    sub = lax.broadcasted_iota(jnp.int32, (n, 128), 0)
    e = jnp.concatenate([g, jnp.zeros((n, 128 - n), F32)], axis=1) + (lane == sub + n).astype(F32)
    for j in range(0, n, nb):
        m = [[None] * nb for _ in range(nb)]
        for r in range(nb):
            for c in range(r, nb):
                m[r][c] = jnp.broadcast_to(e[j + r : j + r + 1, j + c : j + c + 1], (8, 128))
        cols = [jnp.broadcast_to(e[:, j + q : j + q + 1], (n, 128)) for q in range(nb)]
        rows = [jnp.broadcast_to(e[j + q : j + q + 1, :], (8, 128)) for q in range(nb)]
        rec = []
        for q in range(nb):
            rec.append(1.0 / m[q][q])
            low = {r: m[q][r] * rec[q] for r in range(q + 1, nb)}
            for r in range(q + 1, nb):
                for c in range(r, nb):
                    m[r][c] = m[r][c] - low[r] * m[q][c]
                rows[r] = rows[r] - low[r] * rows[q]
                cols[r] = cols[r] - jnp.concatenate([low[r]] * (n // 8), axis=0) * cols[q]
        rows_n = [jnp.concatenate([t] * (n // 8), axis=0) for t in rows]
        out = e
        for q in range(nb):
            out = out - (cols[q] * jnp.concatenate([rec[q]] * (n // 8), axis=0)) * rows_n[q]
        out = jnp.where(sub >= j + nb, out, e)
        for q in range(nb):
            out = jnp.where(sub == j + q, rows_n[q], out)
        e = out
    d = jnp.sum(jnp.where(lane == sub, e, 0.0), axis=1, keepdims=True)
    return e[:, n : 2 * n] * (1.0 / jnp.sqrt(d))


def prepare_kernel(
    prank_ref, crank_ref, trank_ref, krank_ref,
    rows_hbm, cols_hbm, tr_hbm, s_ref, zc_ref, zp_ref, f_hbm,
    w_ref, h_ref, k_ref, ri_ref, q_ref,
    rows_ref, cols_ref, tr_ref, f_ref, load_sem, send_sem, recv_sem, give_sem, take_sem,
):
    row = lax.axis_index("row")
    col = lax.axis_index("col")
    devices = f_ref.shape[0]
    core = lax.rem(row, 2)
    pair = row + 1 - 2 * core
    chips = devices // 2
    tiles, r = zp_ref.shape[0], zp_ref.shape[1]
    width = s_ref.shape[1]
    others = [lax.rem(row + 2 * n, devices) for n in range(1, chips)]
    sources = [lax.rem(row - 2 * n + devices, devices) for n in range(1, chips)]
    barrier = pltpu.get_barrier_semaphore()
    for to in others + [pair]:
        pl.semaphore_signal(barrier, inc=1, device_id=(to, col), device_id_type=MESH)
    loads = [
        pltpu.make_async_copy(cols_hbm, cols_ref, load_sem.at[0]),
        pltpu.make_async_copy(tr_hbm, tr_ref, load_sem.at[1]),
        pltpu.make_async_copy(rows_hbm, rows_ref, load_sem.at[2]),
        pltpu.make_async_copy(f_hbm, f_ref.at[row], load_sem.at[3]),
    ]
    for copy in loads:
        copy.start()
    pl.semaphore_wait(barrier, chips)

    def remote(src, slot, to, ssem, rsem):
        return pltpu.make_async_remote_copy(
            src_ref=src, dst_ref=f_ref.at[slot], send_sem=ssem, recv_sem=rsem,
            device_id=(to, col), device_id_type=MESH,
        )

    sends = [remote(f_hbm, row, to, send_sem.at[n], recv_sem.at[n]) for n, to in enumerate(others)]
    for copy in sends:
        copy.start()
    gives = [remote(f_hbm, row, pair, give_sem.at[chips - 1], take_sem.at[chips - 1])]
    gives[0].start()

    loads[0].wait()
    loads[1].wait()
    s = s_ref[0:LIVE, :]
    big = [cols_ref[t] for t in range(4)]
    for i in range(tiles):
        big += [tr_ref[i, 0, 4 + t] for t in range(4)]
    hk = nt2(s, jnp.concatenate(big, axis=0))
    live = lax.broadcasted_iota(jnp.int32, (LIVE, 4 * r), 0)
    for i in range(tiles):
        k = jnp.where(live < krank_ref[i], hk[:, 0 : 4 * r], 0.0)
        h = jnp.where(live < krank_ref[i], hk[:, (1 + i) * 4 * r : (2 + i) * 4 * r], 0.0)
        keep_t = lax.broadcasted_iota(jnp.int32, (LIVE, r), 1) < trank_ref[i]
        for t in range(4):
            h_ref[i, t] = jnp.where(keep_t, h[:, t * r : (t + 1) * r], 0.0)
            k_ref[i, t] = k[:, t * r : (t + 1) * r]
    loads[2].wait()
    zc = zc_ref[...]
    v = jnp.concatenate(
        [panel_rows_of(rows_ref, i, 4 + t) for i in range(tiles) for t in range(4)], axis=0
    )
    w_all = nt2(v, zc)
    sub = lax.broadcasted_iota(jnp.int32, (LIVE, LIVE), 0)
    lane = lax.broadcasted_iota(jnp.int32, (LIVE, LIVE), 1)
    keeps = []
    for i in range(tiles):
        keeps.append(
            (lax.broadcasted_iota(jnp.int32, (r, r), 0) < prank_ref[i])
            & (lax.broadcasted_iota(jnp.int32, (r, r), 1) < crank_ref[0])
        )
        w0 = jnp.where(keeps[i], w_all[4 * i * r : (4 * i + 1) * r], 0.0)
        w_ref[i, 0] = w0
        left = jnp.concatenate([h_ref[i, 0], -nt(k_ref[i, 0], w0)], axis=1)
        y = nn(left, jnp.concatenate([tr_ref[i, 0, 0], panel_rows_of(rows_ref, i, 0)], axis=0))
        g = nt(y, y) + ((sub == lane) & (sub >= krank_ref[i])).astype(F32)
        ri = root_inverse(g)
        ri_ref[i] = ri
        q_ref[i] = nn(ri, y)
    zp = jnp.concatenate([zp_ref[i] for i in range(tiles)], axis=0)
    zv = nt2(zp, jnp.concatenate([cols_ref[5 + t] for t in range(3)], axis=0))

    for n, source in enumerate(sources):
        remote(f_hbm, source, pair, send_sem.at[n], recv_sem.at[n]).wait_recv()
        gives.append(remote(f_ref.at[source], source, pair, give_sem.at[n], take_sem.at[n]))
        gives[-1].start()
    for n in range(1, chips):
        slot = lax.rem(pair - 2 * n + devices, devices)
        remote(f_hbm, slot, pair, give_sem.at[n - 1], take_sem.at[n - 1]).wait_recv()
    remote(f_hbm, pair, pair, give_sem.at[chips - 1], take_sem.at[chips - 1]).wait_recv()
    loads[3].wait()
    zf = nn(zp, f_ref[...].reshape(width, f_ref.shape[2]))
    for i in range(tiles):
        for t in range(3):
            dw = w_all[(4 * i + 1 + t) * r : (4 * i + 2 + t) * r]
            part = zv[i * r : (i + 1) * r, t * r : (t + 1) * r] - zf[i * r : (i + 1) * r, t * r : (t + 1) * r]
            w_ref[i, 1 + t] = jnp.where(keeps[i], dw + part, 0.0)
    for copy in sends + gives:
        copy.wait_send()


def finish_kernel(
    trank_ref, rows_ref, cols_ref, tr_ref, w_ref, h_ref, k_ref, ri_ref, q_ref, o_ref
):
    tile = pl.program_id(0)
    r = h_ref.shape[3]
    width = q_ref.shape[2]
    keep_t = lax.broadcasted_iota(jnp.int32, (LIVE, r), 1) < trank_ref[tile]
    w0 = w_ref[0, 0]
    dw = [w_ref[0, 1 + t] for t in range(3)]
    ri = ri_ref[0]
    q = q_ref[0]
    h = [h_ref[0, t] for t in range(4)]
    k = jnp.concatenate([k_ref[0, t] for t in range(4)], axis=0)
    kw = nt(k, w0)
    kd = nt(k_ref[0, 0], jnp.concatenate(dw, axis=0))
    left = [jnp.concatenate([h[0], -kw[0:LIVE]], axis=1)]
    for t in range(3):
        left.append(
            jnp.concatenate(
                [h[1 + t], -(kw[(1 + t) * LIVE : (2 + t) * LIVE] + kd[:, t * r : (t + 1) * r])], axis=1
            )
        )
    left = nn(ri, jnp.concatenate(left, axis=1))
    left0 = left[:, 0 : 2 * r]
    ups = [
        jnp.concatenate([tr_ref[0, 0, t], panel_rows_of(rows_ref, 0, t)], axis=0) for t in range(4)
    ]
    e = nn2(jnp.concatenate([left[:, 2 * r * t : 2 * r * (t + 1)] for t in (1, 2, 3)], axis=0), ups[0])
    e = e + jnp.concatenate([nn2(left0, ups[1 + t]) for t in range(3)], axis=0)
    m = nt2(e, q)
    sub = lax.broadcasted_iota(jnp.int32, (LIVE, LIVE), 0)
    lane = lax.broadcasted_iota(jnp.int32, (LIVE, LIVE), 1)
    phi = []
    for t in range(3):
        mt = m[t * LIVE : (t + 1) * LIVE, :]
        mid = mt + mt.T
        phi.append(jnp.where(sub > lane, mid, jnp.where(sub == lane, 0.5 * mid, 0.0)))
    dq = e - nn(jnp.concatenate(phi, axis=0), q)
    qs = jnp.concatenate([q, dq], axis=0)
    js = nt2(qs, ups[0])
    extra = nt2(q, jnp.concatenate(ups[1:], axis=0))
    js = [js[0:LIVE]] + [
        js[(1 + t) * LIVE : (2 + t) * LIVE] + extra[:, 2 * r * t : 2 * r * (t + 1)] for t in range(3)
    ]
    jw = nn(jnp.concatenate([j[:, r:] for j in js], axis=0), w0)
    jd = nn(js[0][:, r:], jnp.concatenate(dw, axis=1))
    ns = []
    for t in range(4):
        b = jw[t * LIVE : (t + 1) * LIVE]
        if t:
            b = b + jd[:, (t - 1) * r : t * r]
        ns.append(jnp.concatenate([jnp.where(keep_t, js[t][:, :r], 0.0), -b], axis=1))
    vs = [jnp.concatenate([tr_ref[0, 0, 4 + t], cols_ref[t]], axis=0) for t in range(4)]
    b = nn2(jnp.concatenate(ns, axis=0), vs[0])
    up_scale = math.sqrt(width)
    down_scale = 1.0 / math.sqrt(r)
    zero = jnp.zeros((r - LIVE, width), F32)
    for t in range(4):
        o_ref[0, 0, t, 0:LIVE, :] = qs[t * LIVE : (t + 1) * LIVE] * up_scale
        bt = b[t * LIVE : (t + 1) * LIVE]
        if t:
            bt = bt + nn2(ns[0], vs[t])
        o_ref[0, 0, 4 + t, 0:LIVE, :] = bt * down_scale
        o_ref[0, 0, t, LIVE:r, :] = zero
        o_ref[0, 0, 4 + t, LIVE:r, :] = zero


def whole(shape):
    return pl.BlockSpec(shape, lambda i: (0,) * len(shape))


def tiled(shape):
    return pl.BlockSpec(shape, lambda i: (i,) + (0,) * (len(shape) - 1))


def params():
    return pltpu.CompilerParams(vmem_limit_bytes=56 << 20)


def cost(flops, nbytes):
    return pl.CostEstimate(flops=int(flops), bytes_accessed=int(nbytes), transcendentals=0)


def on_device(
    diag, panel_rows, panel_cols, trailing, sketch, panel_rank, col_rank, tile_rank, keep_rank
):
    rank, width = sketch.shape
    tiles = trailing.shape[0]
    tile_rank, keep_rank = tile_rank.reshape(-1), keep_rank.reshape(-1)
    pieces = lax.axis_size("col")
    rows = lax.all_gather(panel_rows, "col", axis=0, tiled=False)
    own_cols = panel_cols[0].transpose(1, 0, 2).reshape(-1, width)
    gathered = gather(jnp.concatenate([diag[0], own_cols], axis=0), 1)
    inverse = pl.pallas_call(
        invert_kernel,
        out_shape=jax.ShapeDtypeStruct((width, width), F32),
        scratch_shapes=[
            pltpu.VMEM((BLOCK, BLOCK), F32),
            pltpu.VMEM((width, 3 * BLOCK), BF16),
            pltpu.VMEM((3 * BLOCK, width), BF16),
        ],
        compiler_params=params(),
        cost_estimate=cost(60e9, 8 << 20),
        name="invert",
    )(gathered)
    vmem = pl.BlockSpec(memory_space=pltpu.VMEM)
    hbm = pl.BlockSpec(memory_space=pl.ANY)
    smem = pl.BlockSpec(memory_space=pltpu.SMEM)
    v_spec = pl.BlockSpec(
        (pieces, tiles, 1) + rows.shape[3:], lambda i: (0, 0, 4, 0, 0)
    )
    outs = dict(
        zc=(rank, width),
        zp=(tiles, rank, width),
        f=(diag.shape[1], 3 * rank),
        cols=(panel_cols.shape[1], rank, width),
    )
    zc, zp, f, cols = pl.pallas_call(
        column_kernel,
        grid=(1,),
        in_specs=[whole(gathered.shape), v_spec, whole(inverse.shape), whole(diag.shape)],
        out_specs=[whole(v) for v in outs.values()],
        out_shape=[jax.ShapeDtypeStruct(v, F32) for v in outs.values()],
        compiler_params=params(),
        cost_estimate=cost(2e9, 6 << 20),
        name="columns",
    )(gathered, rows, inverse, diag)
    mids = dict(
        w=(tiles, 4, rank, rank),
        h=(tiles, 4, LIVE, rank),
        k=(tiles, 4, LIVE, rank),
        ri=(tiles, LIVE, LIVE),
        q=(tiles, LIVE, width),
    )
    devices = lax.axis_size("row")
    mid = pl.pallas_call(
        prepare_kernel,
        in_specs=[smem] * 4 + [hbm] * 3 + [vmem] * 3 + [hbm],
        out_specs=[vmem] * len(mids),
        out_shape=[jax.ShapeDtypeStruct(v, F32) for v in mids.values()],
        scratch_shapes=[
            pltpu.VMEM(rows.shape, F32),
            pltpu.VMEM(cols.shape, F32),
            pltpu.VMEM(trailing.shape, F32),
            pltpu.VMEM((devices,) + f.shape, F32),
            pltpu.SemaphoreType.DMA((4,)),
            pltpu.SemaphoreType.DMA((devices // 2 - 1,)),
            pltpu.SemaphoreType.DMA((devices // 2 - 1,)),
            pltpu.SemaphoreType.DMA((devices // 2,)),
            pltpu.SemaphoreType.DMA((devices // 2,)),
        ],
        compiler_params=pltpu.CompilerParams(
            vmem_limit_bytes=56 << 20, collective_id=2, has_side_effects=True
        ),
        cost_estimate=cost(10e9, 20 << 20),
        name="prepare",
    )(panel_rank, col_rank, tile_rank, keep_rank, rows, cols, trailing, sketch, zc, zp, f)
    tr_spec = tiled((1,) + trailing.shape[1:])
    return pl.pallas_call(
        finish_kernel,
        grid=(tiles,),
        in_specs=[
            smem,
            pl.BlockSpec((pieces, 1, 4) + rows.shape[3:], lambda i: (0, i, 0, 0, 0)),
            pl.BlockSpec((4,) + cols.shape[1:], lambda i: (0, 0, 0)),
            tr_spec,
        ]
        + [tiled((1,) + v[1:]) for v in mids.values()],
        out_specs=tr_spec,
        out_shape=jax.ShapeDtypeStruct(trailing.shape, F32),
        compiler_params=params(),
        cost_estimate=cost(10e9, 20 << 20),
        name="finish",
    )(tile_rank, rows, cols, trailing, *mid)


def solution(mesh):
    in_specs = (
        P(None, "row", None),
        P("row", None, None, "col"),
        P("col", None, "row", None),
        P("row", "col", None, None, None),
        P(),
        P("row"),
        P("col"),
        P("row", "col"),
        P("row", "col"),
    )
    out_specs = P("row", "col", None, None, None)
    return jax.shard_map(
        on_device, mesh=mesh, in_specs=in_specs, out_specs=out_specs, check_vma=False
    )
```

```python
import functools
import math

import jax
import jax.numpy as jnp
from jax import lax
from jax.experimental import pallas as pl
from jax.experimental.pallas import tpu as pltpu
from jax.sharding import PartitionSpec as P

HI = lax.Precision.HIGHEST
BLOCK = 128
NPIV = 8
LIVE = 32
F32 = jnp.float32
BF16 = jnp.bfloat16
MESH = pl.DeviceIdType.MESH
SIDE = 4
SENDS = 4 * SIDE + 2 * SIDE + SIDE * SIDE - SIDE + 2 + 2 + 2


def nn(x, y):
    return lax.dot_general(
        x, y, (((1,), (0,)), ((), ())), precision=HI, preferred_element_type=F32
    )


def nt(x, y):
    return lax.dot_general(
        x, y, (((1,), (1,)), ((), ())), precision=HI, preferred_element_type=F32
    )


def total(terms):
    terms = list(terms)
    while len(terms) > 1:
        terms = [
            terms[i] + terms[i + 1] if i + 1 < len(terms) else terms[i]
            for i in range(0, len(terms), 2)
        ]
    return terms[0]


def small_inverse(m):
    n = len(m)
    if n == 1:
        return [[1.0 / m[0][0]]]
    if n == 2:
        r = 1.0 / (m[0][0] * m[1][1] - m[0][1] * m[0][1])
        return [[m[1][1] * r, -m[0][1] * r], [-m[0][1] * r, m[0][0] * r]]
    h = n // 2
    e = small_inverse([row[:h] for row in m[:h]])
    b = [row[h:] for row in m[:h]]
    x = [[total(e[i][k] * b[k][j] for k in range(h)) for j in range(h)] for i in range(h)]
    s = [[None] * h for _ in range(h)]
    for i in range(h):
        for j in range(i, h):
            s[i][j] = m[h + i][h + j] - total(b[k][i] * x[k][j] for k in range(h))
            s[j][i] = s[i][j]
    g = small_inverse(s)
    o = [[-total(x[i][k] * g[k][j] for k in range(h)) for j in range(h)] for i in range(h)]
    t = [[None] * h for _ in range(h)]
    for i in range(h):
        for j in range(i, h):
            t[i][j] = e[i][j] - total(o[i][k] * x[j][k] for k in range(h))
            t[j][i] = t[i][j]
    return [t[i] + o[i] for i in range(h)] + [[o[j][i] for j in range(h)] + g[i] for i in range(h)]


def split3(x):
    a = x.astype(BF16)
    r = x - a.astype(F32)
    b = r.astype(BF16)
    return a, b, (r - b.astype(F32)).astype(BF16)


def left6(parts):
    a, b, c = parts
    return jnp.concatenate([a, b, a, b, a, c], axis=1)


def right6(parts):
    a, b, c = parts
    return jnp.concatenate([a, a, b, b, c, a], axis=0)


def mm(x, y):
    return lax.dot_general(x, y, (((1,), (0,)), ((), ())), preferred_element_type=F32)


def split2(x):
    a = x.astype(BF16)
    return a, (x - a.astype(F32)).astype(BF16)


def nn2(x, y):
    m = x.shape[0]
    a, b = split2(x)
    left = jnp.concatenate([jnp.concatenate([a, a], axis=1), jnp.concatenate([b, b], axis=1)], axis=0)
    r = mm(left, jnp.concatenate(split2(y), axis=0))
    return r[:m] + r[m:]


def nn3(x, y):
    m = x.shape[0]
    a, b, c = split3(x)
    ya, yb, yc = split3(y)
    r = mm(jnp.concatenate([a, b, c], axis=0), ya)
    q = mm(jnp.concatenate([a, b], axis=0), yb)
    return ((r[2 * m :] + mm(a, yc)) + q[m:]) + (r[m : 2 * m] + q[:m]) + r[:m]


def nt2(x, y):
    m, n = x.shape[0], y.shape[0]
    r = lax.dot_general(
        jnp.concatenate(split2(x), axis=0),
        jnp.concatenate(split2(y), axis=0),
        (((1,), (1,)), ((), ())),
        preferred_element_type=F32,
    )
    r = r[:m] + r[m:]
    return r[:, :n] + r[:, n:]


def pivot_steps(d):
    n, half = d.shape[0], NPIV // 2
    sub8 = lax.broadcasted_iota(jnp.int32, (8, n), 0)
    lane8 = lax.broadcasted_iota(jnp.int32, (8, n), 1)
    v = [d[8 * i : 8 * i + 8, :] for i in range(n // 8)]
    for g in range(n // 8):
        j = NPIV * g
        cols = [jnp.broadcast_to(v[g][:, j + q : j + q + 1], (8, n)) for q in range(NPIV)]
        m = [[None] * NPIV for _ in range(NPIV)]
        for r in range(NPIV):
            for c in range(r, NPIV):
                m[r][c] = jnp.broadcast_to(cols[c][r : r + 1, :], (8, n))
                m[c][r] = m[r][c]
        own = (lane8 >= j) & (lane8 < j + NPIV)
        rows = [
            jnp.where(own, (lane8 == j + q).astype(F32), jnp.broadcast_to(v[g][q : q + 1, :], (8, n)))
            for q in range(NPIV)
        ]
        span = range(half)
        e = small_inverse([row[:half] for row in m[:half]])
        b = [row[half:] for row in m[:half]]
        x = [[total(e[i][k] * b[k][q] for k in span) for q in span] for i in span]
        s = [[None] * half for _ in span]
        for i in span:
            for q in range(i, half):
                s[i][q] = m[half + i][half + q] - total(b[k][i] * x[k][q] for k in span)
                s[q][i] = s[i][q]
        f = small_inverse(s)
        top = [total(e[i][k] * rows[k] for k in span) for i in span]
        low = [rows[half + i] - total(b[k][i] * top[k] for k in span) for i in span]
        low = [total(f[i][k] * low[k] for k in span) for i in span]
        new = [top[i] - total(x[i][k] * low[k] for k in span) for i in span] + low
        out = [None] * len(v)
        first = (g + 1) % len(v)
        for i in [first] + [k for k in range(len(v)) if k != first]:
            if i == g:
                t = new[0]
                for q in range(1, NPIV):
                    t = jnp.where(sub8 == q, new[q], t)
            else:
                t = jnp.where(own, 0.0, v[i])
                for q in list(range(half, NPIV)) + list(range(half)):
                    t = t - jnp.broadcast_to(v[i][:, j + q : j + q + 1], (8, n)) * new[q]
            out[i] = t
        v = out
        yield jnp.concatenate(v, axis=0)


def invert(o_ref, p_ref, l_ref, r_ref, between):
    size = o_ref.shape[0]
    blocks = size // BLOCK
    d = None
    for d in pivot_steps(o_ref[0:BLOCK, 0:BLOCK]):
        pass
    p_ref[...] = d

    def step(k, last):
        off = pl.multiple_of(k * BLOCK, BLOCK)
        here = pl.ds(off, BLOCK)
        p = p_ref[...]
        p6 = left6(split3(p))
        for q, part in enumerate(split3(o_ref[:, here])):
            l_ref[:, q * BLOCK : (q + 1) * BLOCK] = part

        def left_of(row):
            return left6([l_ref[pl.ds(row, BLOCK), q * BLOCK : (q + 1) * BLOCK] for q in range(3)])

        steps, found = iter(()), None
        if not last:
            nxt = pl.multiple_of((k + 1) * BLOCK, BLOCK)
            rn = mm(p6, right6(split3(o_ref[here, pl.ds(nxt, BLOCK)])))
            steps = pivot_steps(
                o_ref[pl.ds(nxt, BLOCK), pl.ds(nxt, BLOCK)] - mm(left_of(nxt), right6(split3(rn)))
            )
        o_ref[here, here] = jnp.zeros((BLOCK, BLOCK), F32)
        for h in range(2):
            cs = slice(h * size // 2, (h + 1) * size // 2)
            o_ref[here, cs] = mm(p6, right6(split3(o_ref[here, cs])))
        o_ref[here, here] = p
        for q, part in enumerate(split3(o_ref[here, :])):
            r_ref[q * BLOCK : (q + 1) * BLOCK, :] = part
        for q in range(1, blocks):
            row = pl.multiple_of(lax.rem(k + q, blocks) * BLOCK, BLOCK)
            o_ref[pl.ds(row, BLOCK), here] = jnp.zeros((BLOCK, BLOCK), F32)
            left = left_of(row)
            for h in range(2):
                cs = slice(h * size // 2, (h + 1) * size // 2)
                right = right6([r_ref[q3 * BLOCK : (q3 + 1) * BLOCK, cs] for q3 in range(3)])
                o_ref[pl.ds(row, BLOCK), cs] = o_ref[pl.ds(row, BLOCK), cs] - mm(left, right)
                found = next(steps, found)
        for found in steps:
            pass
        if not last:
            p_ref[...] = found

    def body(k, carry):
        between(k)
        step(k, False)
        return carry

    lax.fori_loop(0, blocks - 1, body, 0)
    step(blocks - 1, True)


def factor_kernel(
    x_ref, panel_ref, o_ref, rows_ref, inv_ref,
    stage_ref, stage2_ref, p_ref, l_ref, r_ref,
    local_sem, send_sem, recv_sem, pair_sem, load_sem, zsend_sem, zrecv_sem,
):
    row = lax.axis_index("row")
    col = lax.axis_index("col")
    core = lax.rem(row, 2)
    x0 = lax.rem(row // 2, SIDE)
    y0 = row // (2 * SIDE)
    half = x_ref.shape[0] // 2

    def device(i1, i2, c=None):
        c = core if c is None else c
        dx = i1 * (1 - core) + i2 * core
        dy = i1 * core + i2 * (1 - core)
        return (lax.rem(y0 + dy + SIDE, SIDE) * SIDE + lax.rem(x0 + dx + SIDE, SIDE)) * 2 + c

    peers = {
        "a+": device(1, 0),
        "a-": device(-1, 0),
        "b+": device(0, 1),
        "b-": device(0, -1),
        "pair": device(0, 0, 1 - core),
    }
    shift = {"a+": (1, 0), "a-": (-1, 0), "b+": (0, 1), "b-": (0, -1)}
    depth = rows_ref.shape[0]
    ahead, back = lax.rem(col + 1, depth), lax.rem(col + depth - 1, depth)
    barrier = pltpu.get_barrier_semaphore()
    for to in peers.values():
        pl.semaphore_signal(barrier, inc=1, device_id=(to, col), device_id_type=MESH)
    for to in (ahead, back):
        pl.semaphore_signal(barrier, inc=1, device_id=(row, to), device_id_type=MESH)
    pl.semaphore_wait(barrier, len(peers) + 2)

    mine = pltpu.make_async_copy(x_ref, stage_ref, local_sem.at[0])
    mine.start()
    mine2 = pltpu.make_async_copy(panel_ref, stage2_ref, local_sem.at[2])
    mine2.start()

    def ring(dist, up, h=None):
        owner = lax.rem(col - dist + depth, depth) if up else lax.rem(col + dist, depth)
        source = panel_ref if dist == 0 else rows_ref.at[owner]
        target = rows_ref.at[owner]
        if h is not None:
            source, target = source.at[h], target.at[h]
        return pltpu.make_async_remote_copy(
            src_ref=source,
            dst_ref=target,
            send_sem=zsend_sem.at[dist, 0 if up else 1],
            recv_sem=zrecv_sem.at[dist, 0 if up else 1],
            device_id=(row, ahead if up else back),
            device_id_type=MESH,
        )

    def landed(dist, up, h=None):
        owner = lax.rem(col - dist - 1 + depth, depth) if up else lax.rem(col + dist + 1, depth)
        target = rows_ref.at[owner]
        if h is not None:
            target = target.at[h]
        pltpu.make_async_remote_copy(
            src_ref=target,
            dst_ref=target,
            send_sem=zsend_sem.at[dist, 0 if up else 1],
            recv_sem=zrecv_sem.at[dist, 0 if up else 1],
            device_id=(row, ahead if up else back),
            device_id_type=MESH,
        ).wait_recv()

    ring(0, True).start()
    ring(0, False).start()
    sent = []

    def part(ref, h):
        return ref if h is None else ref.at[pl.ds(h * half, half)]

    def send(i1, i2, to, h=None):
        owner = device(i1, i2)
        source = x_ref if (i1, i2) == (0, 0) else o_ref.at[owner]
        if to == "pair":
            sem = pair_sem.at[i1 % SIDE, i2 % SIDE]
        else:
            s1, s2 = shift[to]
            sem = recv_sem.at[(i1 - s1) % SIDE, (i2 - s2) % SIDE, h or 0]
        copy = pltpu.make_async_remote_copy(
            src_ref=part(source, h),
            dst_ref=part(o_ref.at[owner], h),
            send_sem=send_sem.at[len(sent)],
            recv_sem=sem,
            device_id=(peers[to], col),
            device_id_type=MESH,
        )
        copy.start()
        sent.append(copy)

    def arrive(i1, i2, h=None, pair=False):
        owner = device(i1, i2)
        sem = pair_sem.at[i1 % SIDE, i2 % SIDE] if pair else recv_sem.at[i1 % SIDE, i2 % SIDE, h or 0]
        dst = part(o_ref.at[owner], h)
        pltpu.make_async_remote_copy(
            src_ref=dst,
            dst_ref=dst,
            send_sem=send_sem.at[0],
            recv_sem=sem,
            device_id=(peers["pair"], col),
            device_id_type=MESH,
        ).wait_recv()

    def spread(i1):
        send(i1, 0, "b+")
        send(i1, 0, "b-")
        send(i1, 0, "pair")

    send(0, 0, "a+")
    send(0, 0, "a-")
    spread(0)
    mine.wait()
    keep = pltpu.make_async_copy(stage_ref, o_ref.at[row], local_sem.at[1])
    keep.start()
    arrive(-1, 0)
    send(-1, 0, "a+", 0)
    spread(-1)
    arrive(1, 0)
    send(1, 0, "a-", 1)
    spread(1)
    arrive(2, 0, 0)
    arrive(2, 0, 1)
    spread(2)
    order = (0, -1, 1, 2)
    for i1 in order:
        arrive(i1, -1)
        send(i1, -1, "b+", 0)
        send(i1, -1, "pair")
        arrive(i1, 1)
        send(i1, 1, "b-", 1)
        send(i1, 1, "pair")
    for i1 in order:
        arrive(i1, 2, 0)
        arrive(i1, 2, 1)
        send(i1, 2, "pair")
    for i1 in range(SIDE):
        for i2 in range(SIDE):
            arrive_pair(o_ref, device, pair_sem, send_sem, i1, i2, core, peers["pair"], col)
    for copy in sent:
        copy.wait_send()
    keep.wait()
    mine2.wait()
    keep2 = pltpu.make_async_copy(stage2_ref, rows_ref.at[col], local_sem.at[3])
    keep2.start()
    landed(0, True)
    landed(0, False)
    ring(1, True).start()
    ring(1, False).start()
    devices = o_ref.shape[0]
    share = inv_ref.shape[0] // devices
    loads = [
        pltpu.make_async_copy(
            o_ref.at[i, pl.ds(0, share)], inv_ref.at[pl.ds(i * share, share)], load_sem.at[i]
        )
        for i in range(devices)
    ]
    for copy in loads:
        copy.start()
    for copy in loads:
        copy.wait()

    def between(k):
        @pl.when(k == 2)
        def _():
            landed(1, True)
            landed(1, False)
            ring(2, True).start()
            ring(2, False).start()

        @pl.when(k == 4)
        def _():
            landed(2, True)
            landed(2, False)
            ring(3, True, 0).start()
            ring(3, False, 1).start()

    invert(inv_ref, p_ref, l_ref, r_ref, between)
    landed(3, True, 0)
    landed(3, False, 1)
    for dist in range(4):
        ring(dist, True, 0 if dist == 3 else None).wait_send()
        ring(dist, False, 1 if dist == 3 else None).wait_send()
    keep2.wait()


def arrive_pair(o_ref, device, pair_sem, send_sem, i1, i2, core, pair, col):
    owner = device(i2, i1, 1 - core)
    pltpu.make_async_remote_copy(
        src_ref=o_ref.at[owner],
        dst_ref=o_ref.at[owner],
        send_sem=send_sem.at[0],
        recv_sem=pair_sem.at[i1, i2],
        device_id=(pair, col),
        device_id_type=MESH,
    ).wait_recv()


def column_kernel(g_ref, rows_ref, inv_ref, diag_ref, zc_ref, zp_ref, f_ref, c_ref):
    devices, extent, width = g_ref.shape
    share = width // devices
    for i in range(devices):
        for j in range((extent - share) // 8):
            c_ref[:, i * ((extent - share) // 8) + j, :] = g_ref[i, share + 8 * j : share + 8 * (j + 1), :]
    tiles = rows_ref.shape[1]
    v = jnp.concatenate([c_ref[4]] + [panel_rows_of(rows_ref, t, 0) for t in range(tiles)], axis=0)
    z = nn3(v, inv_ref[...])
    r = zc_ref.shape[0]
    zc_ref[...] = z[:r]
    for t in range(tiles):
        zp_ref[t] = z[(1 + t) * r : (2 + t) * r]
    f = nt(diag_ref[1:4].reshape(3 * share, width), z[:r])
    f_ref[...] = jnp.concatenate([f[t * share : (t + 1) * share] for t in range(3)], axis=1)


def panel_rows_of(ref, tile, comp):
    return jnp.concatenate([ref[piece, tile, comp] for piece in range(ref.shape[0])], axis=1)


def root_inverse(g):
    n, nb = LIVE, 4
    lane = lax.broadcasted_iota(jnp.int32, (n, 128), 1)
    sub = lax.broadcasted_iota(jnp.int32, (n, 128), 0)
    e = jnp.concatenate([g, jnp.zeros((n, 128 - n), F32)], axis=1) + (lane == sub + n).astype(F32)
    for j in range(0, n, nb):
        m = [[None] * nb for _ in range(nb)]
        for r in range(nb):
            for c in range(r, nb):
                m[r][c] = jnp.broadcast_to(e[j + r : j + r + 1, j + c : j + c + 1], (8, 128))
        cols = [jnp.broadcast_to(e[:, j + q : j + q + 1], (n, 128)) for q in range(nb)]
        rows = [jnp.broadcast_to(e[j + q : j + q + 1, :], (8, 128)) for q in range(nb)]
        rec = []
        for q in range(nb):
            rec.append(1.0 / m[q][q])
            low = {r: m[q][r] * rec[q] for r in range(q + 1, nb)}
            for r in range(q + 1, nb):
                for c in range(r, nb):
                    m[r][c] = m[r][c] - low[r] * m[q][c]
                rows[r] = rows[r] - low[r] * rows[q]
                cols[r] = cols[r] - jnp.concatenate([low[r]] * (n // 8), axis=0) * cols[q]
        rows_n = [jnp.concatenate([t] * (n // 8), axis=0) for t in rows]
        out = e
        for q in range(nb):
            out = out - (cols[q] * jnp.concatenate([rec[q]] * (n // 8), axis=0)) * rows_n[q]
        out = jnp.where(sub >= j + nb, out, e)
        for q in range(nb):
            out = jnp.where(sub == j + q, rows_n[q], out)
        e = out
    d = jnp.sum(jnp.where(lane == sub, e, 0.0), axis=1, keepdims=True)
    return e[:, n : 2 * n] * (1.0 / jnp.sqrt(d))


def prepare_kernel(
    prank_ref, crank_ref, trank_ref, krank_ref,
    rows_hbm, cols_hbm, tr_hbm, s_ref, zc_ref, zp_ref, f_hbm,
    w_ref, h_ref, k_ref, ri_ref, q_ref,
    rows_ref, cols_ref, tr_ref, f_ref, load_sem, send_sem, recv_sem, give_sem, take_sem,
):
    row = lax.axis_index("row")
    col = lax.axis_index("col")
    devices = f_ref.shape[0]
    core = lax.rem(row, 2)
    pair = row + 1 - 2 * core
    chips = devices // 2
    tiles, r = zp_ref.shape[0], zp_ref.shape[1]
    width = s_ref.shape[1]
    others = [lax.rem(row + 2 * n, devices) for n in range(1, chips)]
    sources = [lax.rem(row - 2 * n + devices, devices) for n in range(1, chips)]
    barrier = pltpu.get_barrier_semaphore()
    for to in others + [pair]:
        pl.semaphore_signal(barrier, inc=1, device_id=(to, col), device_id_type=MESH)
    loads = [
        pltpu.make_async_copy(cols_hbm, cols_ref, load_sem.at[0]),
        pltpu.make_async_copy(tr_hbm, tr_ref, load_sem.at[1]),
        pltpu.make_async_copy(rows_hbm, rows_ref, load_sem.at[2]),
        pltpu.make_async_copy(f_hbm, f_ref.at[row], load_sem.at[3]),
    ]
    for copy in loads:
        copy.start()
    pl.semaphore_wait(barrier, chips)

    def remote(src, slot, to, ssem, rsem):
        return pltpu.make_async_remote_copy(
            src_ref=src, dst_ref=f_ref.at[slot], send_sem=ssem, recv_sem=rsem,
            device_id=(to, col), device_id_type=MESH,
        )

    sends = [remote(f_hbm, row, to, send_sem.at[n], recv_sem.at[n]) for n, to in enumerate(others)]
    for copy in sends:
        copy.start()
    gives = [remote(f_hbm, row, pair, give_sem.at[chips - 1], take_sem.at[chips - 1])]
    gives[0].start()

    loads[0].wait()
    loads[1].wait()
    s = s_ref[0:LIVE, :]
    big = [cols_ref[t] for t in range(4)]
    for i in range(tiles):
        big += [tr_ref[i, 0, 4 + t] for t in range(4)]
    hk = nt2(s, jnp.concatenate(big, axis=0))
    live = lax.broadcasted_iota(jnp.int32, (LIVE, 4 * r), 0)
    for i in range(tiles):
        k = jnp.where(live < krank_ref[i], hk[:, 0 : 4 * r], 0.0)
        h = jnp.where(live < krank_ref[i], hk[:, (1 + i) * 4 * r : (2 + i) * 4 * r], 0.0)
        keep_t = lax.broadcasted_iota(jnp.int32, (LIVE, r), 1) < trank_ref[i]
        for t in range(4):
            h_ref[i, t] = jnp.where(keep_t, h[:, t * r : (t + 1) * r], 0.0)
            k_ref[i, t] = k[:, t * r : (t + 1) * r]
    loads[2].wait()
    zc = zc_ref[...]
    v = jnp.concatenate(
        [panel_rows_of(rows_ref, i, 4 + t) for i in range(tiles) for t in range(4)], axis=0
    )
    w_all = nt2(v, zc)
    sub = lax.broadcasted_iota(jnp.int32, (LIVE, LIVE), 0)
    lane = lax.broadcasted_iota(jnp.int32, (LIVE, LIVE), 1)
    keeps = []
    for i in range(tiles):
        keeps.append(
            (lax.broadcasted_iota(jnp.int32, (r, r), 0) < prank_ref[i])
            & (lax.broadcasted_iota(jnp.int32, (r, r), 1) < crank_ref[0])
        )
        w0 = jnp.where(keeps[i], w_all[4 * i * r : (4 * i + 1) * r], 0.0)
        w_ref[i, 0] = w0
        left = jnp.concatenate([h_ref[i, 0], -nt(k_ref[i, 0], w0)], axis=1)
        y = nn(left, jnp.concatenate([tr_ref[i, 0, 0], panel_rows_of(rows_ref, i, 0)], axis=0))
        g = nt(y, y) + ((sub == lane) & (sub >= krank_ref[i])).astype(F32)
        ri = root_inverse(g)
        ri_ref[i] = ri
        q_ref[i] = nn(ri, y)
    zp = jnp.concatenate([zp_ref[i] for i in range(tiles)], axis=0)
    zv = nt2(zp, jnp.concatenate([cols_ref[5 + t] for t in range(3)], axis=0))

    for n, source in enumerate(sources):
        remote(f_hbm, source, pair, send_sem.at[n], recv_sem.at[n]).wait_recv()
        gives.append(remote(f_ref.at[source], source, pair, give_sem.at[n], take_sem.at[n]))
        gives[-1].start()
    for n in range(1, chips):
        slot = lax.rem(pair - 2 * n + devices, devices)
        remote(f_hbm, slot, pair, give_sem.at[n - 1], take_sem.at[n - 1]).wait_recv()
    remote(f_hbm, pair, pair, give_sem.at[chips - 1], take_sem.at[chips - 1]).wait_recv()
    loads[3].wait()
    zf = nn(zp, f_ref[...].reshape(width, f_ref.shape[2]))
    for i in range(tiles):
        for t in range(3):
            dw = w_all[(4 * i + 1 + t) * r : (4 * i + 2 + t) * r]
            part = zv[i * r : (i + 1) * r, t * r : (t + 1) * r] - zf[i * r : (i + 1) * r, t * r : (t + 1) * r]
            w_ref[i, 1 + t] = jnp.where(keeps[i], dw + part, 0.0)
    for copy in sends + gives:
        copy.wait_send()


def finish_kernel(
    trank_ref, rows_ref, cols_ref, tr_ref, w_ref, h_ref, k_ref, ri_ref, q_ref, o_ref
):
    tile = pl.program_id(0)
    r = h_ref.shape[3]
    width = q_ref.shape[2]
    keep_t = lax.broadcasted_iota(jnp.int32, (LIVE, r), 1) < trank_ref[tile]
    w0 = w_ref[0, 0]
    dw = [w_ref[0, 1 + t] for t in range(3)]
    ri = ri_ref[0]
    q = q_ref[0]
    h = [h_ref[0, t] for t in range(4)]
    k = jnp.concatenate([k_ref[0, t] for t in range(4)], axis=0)
    kw = nt(k, w0)
    kd = nt(k_ref[0, 0], jnp.concatenate(dw, axis=0))
    left = [jnp.concatenate([h[0], -kw[0:LIVE]], axis=1)]
    for t in range(3):
        left.append(
            jnp.concatenate(
                [h[1 + t], -(kw[(1 + t) * LIVE : (2 + t) * LIVE] + kd[:, t * r : (t + 1) * r])], axis=1
            )
        )
    left = nn(ri, jnp.concatenate(left, axis=1))
    left0 = left[:, 0 : 2 * r]
    ups = [
        jnp.concatenate([tr_ref[0, 0, t], panel_rows_of(rows_ref, 0, t)], axis=0) for t in range(4)
    ]
    e = nn2(jnp.concatenate([left[:, 2 * r * t : 2 * r * (t + 1)] for t in (1, 2, 3)], axis=0), ups[0])
    e = e + jnp.concatenate([nn2(left0, ups[1 + t]) for t in range(3)], axis=0)
    m = nt2(e, q)
    sub = lax.broadcasted_iota(jnp.int32, (LIVE, LIVE), 0)
    lane = lax.broadcasted_iota(jnp.int32, (LIVE, LIVE), 1)
    phi = []
    for t in range(3):
        mt = m[t * LIVE : (t + 1) * LIVE, :]
        mid = mt + mt.T
        phi.append(jnp.where(sub > lane, mid, jnp.where(sub == lane, 0.5 * mid, 0.0)))
    dq = e - nn(jnp.concatenate(phi, axis=0), q)
    qs = jnp.concatenate([q, dq], axis=0)
    js = nt2(qs, ups[0])
    extra = nt2(q, jnp.concatenate(ups[1:], axis=0))
    js = [js[0:LIVE]] + [
        js[(1 + t) * LIVE : (2 + t) * LIVE] + extra[:, 2 * r * t : 2 * r * (t + 1)] for t in range(3)
    ]
    jw = nn(jnp.concatenate([j[:, r:] for j in js], axis=0), w0)
    jd = nn(js[0][:, r:], jnp.concatenate(dw, axis=1))
    ns = []
    for t in range(4):
        b = jw[t * LIVE : (t + 1) * LIVE]
        if t:
            b = b + jd[:, (t - 1) * r : t * r]
        ns.append(jnp.concatenate([jnp.where(keep_t, js[t][:, :r], 0.0), -b], axis=1))
    vs = [jnp.concatenate([tr_ref[0, 0, 4 + t], cols_ref[t]], axis=0) for t in range(4)]
    b = nn2(jnp.concatenate(ns, axis=0), vs[0])
    up_scale = math.sqrt(width)
    down_scale = 1.0 / math.sqrt(r)
    zero = jnp.zeros((r - LIVE, width), F32)
    for t in range(4):
        o_ref[0, 0, t, 0:LIVE, :] = qs[t * LIVE : (t + 1) * LIVE] * up_scale
        bt = b[t * LIVE : (t + 1) * LIVE]
        if t:
            bt = bt + nn2(ns[0], vs[t])
        o_ref[0, 0, 4 + t, 0:LIVE, :] = bt * down_scale
        o_ref[0, 0, t, LIVE:r, :] = zero
        o_ref[0, 0, 4 + t, LIVE:r, :] = zero


def whole(shape):
    return pl.BlockSpec(shape, lambda i: (0,) * len(shape))


def tiled(shape):
    return pl.BlockSpec(shape, lambda i: (i,) + (0,) * (len(shape) - 1))


def params():
    return pltpu.CompilerParams(vmem_limit_bytes=56 << 20)


def cost(flops, nbytes):
    return pl.CostEstimate(flops=int(flops), bytes_accessed=int(nbytes), transcendentals=0)


def on_device(
    diag, panel_rows, panel_cols, trailing, sketch, panel_rank, col_rank, tile_rank, keep_rank
):
    rank, width = sketch.shape
    tiles = trailing.shape[0]
    tile_rank, keep_rank = tile_rank.reshape(-1), keep_rank.reshape(-1)
    pieces = lax.axis_size("col")
    own_cols = panel_cols[0].transpose(1, 0, 2).reshape(-1, width)
    block = jnp.concatenate([diag[0], own_cols], axis=0)
    devices = lax.axis_size("row")
    gathered, rows, inverse = pl.pallas_call(
        factor_kernel,
        in_specs=[pl.BlockSpec(memory_space=pl.ANY)] * 2,
        out_specs=[pl.BlockSpec(memory_space=pl.ANY)] * 2 + [pl.BlockSpec(memory_space=pltpu.VMEM)],
        out_shape=[
            jax.ShapeDtypeStruct((devices,) + block.shape, F32),
            jax.ShapeDtypeStruct((pieces,) + panel_rows.shape, F32),
            jax.ShapeDtypeStruct((width, width), F32),
        ],
        scratch_shapes=[
            pltpu.VMEM(block.shape, F32),
            pltpu.VMEM(panel_rows.shape, F32),
            pltpu.VMEM((BLOCK, BLOCK), F32),
            pltpu.VMEM((width, 3 * BLOCK), BF16),
            pltpu.VMEM((3 * BLOCK, width), BF16),
            pltpu.SemaphoreType.DMA((4,)),
            pltpu.SemaphoreType.DMA((SENDS,)),
            pltpu.SemaphoreType.DMA((SIDE, SIDE, 2)),
            pltpu.SemaphoreType.DMA((SIDE, SIDE)),
            pltpu.SemaphoreType.DMA((devices,)),
            pltpu.SemaphoreType.DMA((4, 2)),
            pltpu.SemaphoreType.DMA((4, 2)),
        ],
        compiler_params=pltpu.CompilerParams(
            vmem_limit_bytes=56 << 20, collective_id=1, has_side_effects=True
        ),
        cost_estimate=cost(60e9, 30 << 20),
        name="factor",
    )(block, panel_rows)
    vmem = pl.BlockSpec(memory_space=pltpu.VMEM)
    hbm = pl.BlockSpec(memory_space=pl.ANY)
    smem = pl.BlockSpec(memory_space=pltpu.SMEM)
    v_spec = pl.BlockSpec(
        (pieces, tiles, 1) + rows.shape[3:], lambda i: (0, 0, 4, 0, 0)
    )
    outs = dict(
        zc=(rank, width),
        zp=(tiles, rank, width),
        f=(diag.shape[1], 3 * rank),
        cols=(panel_cols.shape[1], rank, width),
    )
    zc, zp, f, cols = pl.pallas_call(
        column_kernel,
        grid=(1,),
        in_specs=[whole(gathered.shape), v_spec, whole(inverse.shape), whole(diag.shape)],
        out_specs=[whole(v) for v in outs.values()],
        out_shape=[jax.ShapeDtypeStruct(v, F32) for v in outs.values()],
        compiler_params=params(),
        cost_estimate=cost(2e9, 6 << 20),
        name="columns",
    )(gathered, rows, inverse, diag)
    mids = dict(
        w=(tiles, 4, rank, rank),
        h=(tiles, 4, LIVE, rank),
        k=(tiles, 4, LIVE, rank),
        ri=(tiles, LIVE, LIVE),
        q=(tiles, LIVE, width),
    )
    mid = pl.pallas_call(
        prepare_kernel,
        in_specs=[smem] * 4 + [hbm] * 3 + [vmem] * 3 + [hbm],
        out_specs=[vmem] * len(mids),
        out_shape=[jax.ShapeDtypeStruct(v, F32) for v in mids.values()],
        scratch_shapes=[
            pltpu.VMEM(rows.shape, F32),
            pltpu.VMEM(cols.shape, F32),
            pltpu.VMEM(trailing.shape, F32),
            pltpu.VMEM((devices,) + f.shape, F32),
            pltpu.SemaphoreType.DMA((4,)),
            pltpu.SemaphoreType.DMA((devices // 2 - 1,)),
            pltpu.SemaphoreType.DMA((devices // 2 - 1,)),
            pltpu.SemaphoreType.DMA((devices // 2,)),
            pltpu.SemaphoreType.DMA((devices // 2,)),
        ],
        compiler_params=pltpu.CompilerParams(
            vmem_limit_bytes=56 << 20, collective_id=2, has_side_effects=True
        ),
        cost_estimate=cost(10e9, 20 << 20),
        name="prepare",
    )(panel_rank, col_rank, tile_rank, keep_rank, rows, cols, trailing, sketch, zc, zp, f)
    tr_spec = tiled((1,) + trailing.shape[1:])
    return pl.pallas_call(
        finish_kernel,
        grid=(tiles,),
        in_specs=[
            smem,
            pl.BlockSpec((pieces, 1, 4) + rows.shape[3:], lambda i: (0, i, 0, 0, 0)),
            pl.BlockSpec((4,) + cols.shape[1:], lambda i: (0, 0, 0)),
            tr_spec,
        ]
        + [tiled((1,) + v[1:]) for v in mids.values()],
        out_specs=tr_spec,
        out_shape=jax.ShapeDtypeStruct(trailing.shape, F32),
        compiler_params=params(),
        cost_estimate=cost(10e9, 20 << 20),
        name="finish",
    )(tile_rank, rows, cols, trailing, *mid)


def solution(mesh):
    in_specs = (
        P(None, "row", None),
        P("row", None, None, "col"),
        P("col", None, "row", None),
        P("row", "col", None, None, None),
        P(),
        P("row"),
        P("col"),
        P("row", "col"),
        P("row", "col"),
    )
    out_specs = P("row", "col", None, None, None)
    return jax.shard_map(
        on_device, mesh=mesh, in_specs=in_specs, out_specs=out_specs, check_vma=False
    )
```
